128 devices in a mesh: docs: 128 (over y, x, z, core).
Axes of the slice: x: 4, y: 4, z: 4, core: 2. Of those that a mesh axis runs over, the one named last changes fastest.
Arguments:
- block_count_values: int32 [5120, 256, 256], P('docs'), may hold values from 1 to 15
- word_factor: bfloat16 [262144, 512], P('docs'), may hold values from 0.029907227 to 0.29882812
- doc_factor: bfloat16 [512, 262144], P(None, 'docs'), may hold values from 0.029907227 to 0.29882812
- block_word: int32 [5120], P('docs'), may hold values from 0 to 1023, as said below
- block_docs: int32 [5120], P('docs'), may hold values from 0 to 7
- block_count: int32 [128], P('docs'), may hold values from 5 to 40
Outputs:
- word_gradient: float32 [262144, 512], P('docs')
- document_gradient: float32 [512, 262144], P(None, 'docs')
The draws below stay inside these ranges and needn't reach their ends.
Inputs may be any that keep to these rules, and one draw needn't show every extreme that they name: `block_word`: on device d every slot names a word block from (d - 1) * 8 to (d + 2) * 8 - 1, taken modulo 1024; the pairs of word block and document block of one device's slots are all different.
All inputs are finite; a program needn't handle non-finite values.
Results may differ from the reference program's by a relative error of at most 0.00038.
Values may be sent and summed in bfloat16 or wider, within the bound.
No kernel may reach another device: no remote copies, remote signals or barrier semaphores. Data moves between devices by JAX's collectives and lax.ppermute only.
A program may use at most 128 MiB of HBM per device.

```python
import math
import jax
import jax.numpy as jnp
from jax import lax

K = 512
BLOCK_EDGE = 256
WBD = 8
DBD = 8
NB_CAP = 40
WORDS = 262144
DOCS = 262144
SLOT_COUNT = 5120
N_DOCS = 128


def slot_pairs(key):
    keys = jax.random.split(jax.random.fold_in(key, 7), N_DOCS)
    orders = jax.vmap(lambda one_key: jax.random.permutation(one_key, 3 * WBD * DBD))(keys)[:, :NB_CAP]
    owners = jnp.arange(N_DOCS, dtype=jnp.int32)[:, None]
    words = jnp.mod((owners - 1) * WBD + orders // DBD, WBD * N_DOCS)
    return (words.reshape(-1).astype(jnp.int32), (orders % DBD).reshape(-1).astype(jnp.int32))


def draw_block_word(key, part):
    return slot_pairs(key)[0]


def draw_block_docs(key, part):
    return slot_pairs(key)[1]


def draw_block_count(key, part):
    lowest = max(1, NB_CAP // 8)
    counts = jax.random.randint(jax.random.fold_in(key, 11), (N_DOCS,), lowest, NB_CAP + 1)
    busiest = jax.random.randint(jax.random.fold_in(key, 13), (), 0, N_DOCS)
    return counts.at[busiest].set(NB_CAP).astype(jnp.int32)


def with_ends(values, rng, smallest, largest):
    spot = [jax.random.randint(jax.random.fold_in(rng, axis), (), 0, length) for axis, length in enumerate(values.shape)]
    main_axis = values.shape.index(max(values.shape))
    beside = spot[:main_axis] + [(spot[main_axis] + 1) % values.shape[main_axis]] + spot[main_axis + 1:]
    return values.at[tuple(spot)].set(smallest).at[tuple(beside)].set(largest)


def block_levels(key, extent, cuts, least, largest):
    gain = 1.0
    for dim, blocks in cuts:
        steps = jax.random.uniform(jax.random.fold_in(jax.random.fold_in(key, 6), dim), (blocks,), jnp.float32, least / len(cuts), largest / len(cuts))
        gain = gain * jnp.repeat(jnp.exp(steps), extent[dim] // blocks).reshape((-1,) + (1,) * (len(extent) - 1 - dim))
    return gain


def setup_inputs(seed: int = 0) -> dict:
    seeds = jax.random.split(jax.random.key(seed), 7)
    block_count_values = with_ends(jax.random.randint(seeds[0], (SLOT_COUNT, BLOCK_EDGE, BLOCK_EDGE), 1, 16), jax.random.fold_in(seeds[0], 1), 1, 15).astype(jnp.int32)
    word_factor = jnp.clip(jnp.exp(math.log(0.29882812) - 2.30176843 * jax.random.uniform(seeds[1], (WORDS, K), jnp.float32) ** block_levels(seeds[1], (WORDS, K), ((0, 128),), -0.2, 0.2)), 0.029907227, 0.29882812).astype(jnp.bfloat16)
    doc_factor = jnp.clip(jnp.exp(math.log(0.29882812) - 2.30176843 * jax.random.uniform(seeds[2], (K, DOCS), jnp.float32) ** block_levels(seeds[2], (K, DOCS), ((1, 128),), -0.2, 0.2)), 0.029907227, 0.29882812).astype(jnp.bfloat16)
    block_word = draw_block_word(jax.random.fold_in(seeds[6], 71), 0)
    block_docs = draw_block_docs(jax.random.fold_in(seeds[6], 71), 0)
    block_count = draw_block_count(jax.random.fold_in(seeds[6], 71), 0)
    return dict(block_count_values=block_count_values, word_factor=word_factor, doc_factor=doc_factor, block_word=block_word, block_docs=block_docs, block_count=block_count)


def reference(block_count_values, word_factor, doc_factor, block_word, block_docs, block_count):
    slot_number = block_count_values.shape[0]
    word_gradient = jnp.zeros(word_factor.shape, jnp.float32)
    document_gradient = jnp.zeros(doc_factor.shape, jnp.float32)

    def step_forward(carry, slot):
        grad_w, grad_h = carry
        device = (slot // NB_CAP).astype(jnp.int32)
        live = (slot % NB_CAP) < block_count[device]
        word_start = (block_word[slot] * BLOCK_EDGE).astype(jnp.int32)
        doc_start = ((device * DBD + block_docs[slot]) * BLOCK_EDGE).astype(jnp.int32)
        word_rows = lax.dynamic_slice_in_dim(word_factor, word_start, BLOCK_EDGE, 0)
        doc_cols = lax.dynamic_slice_in_dim(doc_factor, doc_start, BLOCK_EDGE, 1)
        product = jnp.dot(word_rows, doc_cols, preferred_element_type=jnp.float32)
        counts = lax.dynamic_index_in_dim(block_count_values, slot, 0, keepdims=False).astype(jnp.float32)
        excess = jnp.where(live, 1.0 - counts / product, jnp.zeros_like(product)).astype(jnp.bfloat16)
        term_w = jnp.dot(excess, doc_cols.T, preferred_element_type=jnp.float32)
        term_h = jnp.dot(word_rows.T, excess, preferred_element_type=jnp.float32)
        old_w = lax.dynamic_slice_in_dim(grad_w, word_start, BLOCK_EDGE, 0)
        grad_w = lax.dynamic_update_slice_in_dim(grad_w, old_w + term_w, word_start, 0)
        old_h = lax.dynamic_slice_in_dim(grad_h, doc_start, BLOCK_EDGE, 1)
        grad_h = lax.dynamic_update_slice_in_dim(grad_h, old_h + term_h, doc_start, 1)
        return (grad_w, grad_h), None

    (word_gradient, document_gradient), unused_item = lax.scan(step_forward, (word_gradient, document_gradient), jnp.arange(slot_number, dtype=jnp.int32))
    return word_gradient, document_gradient
```

```python
import functools

import jax
import jax.numpy as jnp
from jax import lax
from jax.experimental import pallas as pl
from jax.experimental.pallas import tpu as pltpu
from jax.sharding import PartitionSpec as P

F32 = jnp.float32
BF16 = jnp.bfloat16
VMEM = pl.BlockSpec(memory_space=pltpu.VMEM)
SMEM = pl.BlockSpec(memory_space=pltpu.SMEM)
ANY = pl.BlockSpec(memory_space=pl.ANY)
DEAD = 1 << 10


def slot_kernel(spec, order, bounds, counts, words, docs, *refs):
    edge, first_group, last_group, base, do_w, do_h, carried = spec
    refs = list(refs)
    grad_h_in = refs.pop(0) if carried else None
    grad_w = refs.pop(0) if do_w else None
    grad_h = refs.pop(0) if do_h else None
    held, sems = refs
    first, last = bounds[first_group], bounds[last_group]

    def fetch(place):
        slot = order[place] & 63
        return pltpu.make_async_copy(counts.at[slot], held.at[place], sems.at[place])

    @pl.loop(first, last)
    def _(place):
        fetch(place).start()

    if do_w:
        grad_w[...] = jnp.zeros_like(grad_w)
    if do_h:
        grad_h[...] = grad_h_in[...] if carried else jnp.zeros_like(grad_h)

    def where_is(place):
        code = order[place]
        word = ((code >> 6) & 15) - base
        doc = code >> 10
        return (
            pl.ds(pl.multiple_of(word * edge, edge), edge),
            pl.ds(pl.multiple_of(doc * edge, edge), edge),
        )

    def product(rows, cols):
        return jnp.dot(words[rows, :], docs[:, cols], preferred_element_type=F32)

    def term_w(excess, cols):
        return lax.dot_general(
            excess, docs[:, cols], (((1,), (1,)), ((), ())), preferred_element_type=F32
        )

    def term_h(excess, rows):
        return lax.dot_general(
            words[rows, :], excess, (((0,), (0,)), ((), ())), preferred_element_type=F32
        )

    @pl.loop(0, (last - first + 1) // 2)
    def _(pair):
        one = first + 2 * pair
        two = jnp.minimum(one + 1, last - 1)
        paired = one + 1 < last
        fetch(one).wait()

        @pl.when(paired)
        def _():
            fetch(two).wait()

        rows_one, cols_one = where_is(one)
        rows_two, cols_two = where_is(two)
        product_one = product(rows_one, cols_one)
        product_two = product(rows_two, cols_two)
        excess_one = (1.0 - held[one].astype(F32) / product_one).astype(BF16)
        excess_two = jnp.where(paired, 1.0 - held[two].astype(F32) / product_two, 0.0).astype(BF16)
        if do_w:
            term_w_one = term_w(excess_one, cols_one)
            term_w_two = term_w(excess_two, cols_two)
        if do_h:
            term_h_one = term_h(excess_one, rows_one)
            term_h_two = term_h(excess_two, rows_two)
        if do_w:
            grad_w[rows_one, :] += term_w_one
            grad_w[rows_two, :] += term_w_two
        if do_h:
            grad_h[:, cols_one] += term_h_one
            grad_h[:, cols_two] += term_h_two


def slots(name, order, bounds, counts, words, docs, groups, base, do_w, do_h, grad_h=None):
    edge = counts.shape[1]
    carried = grad_h is not None
    spec = (edge, groups[0], groups[1], base, do_w, do_h, carried)
    operands = [order, bounds, counts, words, docs] + ([grad_h] if carried else [])
    shapes = []
    if do_w:
        shapes.append(jax.ShapeDtypeStruct(words.shape, F32))
    if do_h:
        shapes.append(jax.ShapeDtypeStruct(docs.shape, F32))
    share = (groups[1] - groups[0]) / 24 * counts.shape[0]
    flops = int(share * 2 * edge * edge * words.shape[1] * (1 + do_w + do_h))
    return pl.pallas_call(
        functools.partial(slot_kernel, spec),
        out_shape=shapes,
        in_specs=[SMEM, SMEM, ANY, VMEM, VMEM] + ([VMEM] if carried else []),
        out_specs=[VMEM] * len(shapes),
        scratch_shapes=[
            pltpu.VMEM(counts.shape, counts.dtype),
            pltpu.SemaphoreType.DMA((counts.shape[0],)),
        ],
        input_output_aliases={5: int(do_w)} if carried else {},
        compiler_params=pltpu.CompilerParams(vmem_limit_bytes=48 << 20),
        cost_estimate=pl.CostEstimate(
            flops=1, bytes_accessed=1, transcendentals=0
        ),
        name=name,
    )(*operands)


def slot_order(block_word, block_docs, live, position, own_blocks, devices):
    slot = jnp.arange(block_word.shape[0], dtype=jnp.int32)
    local = jnp.mod(block_word - (position - 1) * own_blocks, own_blocks * devices)
    side = local // own_blocks
    inner = local - side * own_blocks
    even = position % 2 == 0
    group = jnp.where(side == 1, 0, jnp.where((side == 0) == even, 2, 1))
    key = jnp.where(slot < live, group * own_blocks + inner, DEAD)
    rank_key = key * 64 + slot
    rank = jnp.sum((rank_key[None, :] < rank_key[:, None]).astype(jnp.int32), axis=1)
    code = slot + inner * 64 + block_docs * 1024
    order = jnp.sum(jnp.where(rank[:, None] == slot[None, :], code[:, None], 0), axis=0)
    marks = jnp.arange(3 * own_blocks + 1, dtype=jnp.int32)
    bounds = jnp.sum((key[None, :] < marks[:, None]).astype(jnp.int32), axis=1)
    return order, bounds


def on_device(block_count_values, word_factor, doc_factor, block_word, block_docs, block_count):
    devices = lax.axis_size("docs")
    position = lax.axis_index("docs")
    edge = block_count_values.shape[1]
    rows = word_factor.shape[0]
    own_blocks = rows // edge
    half = rows // 2
    half_blocks = own_blocks // 2
    partner_route = [(i, i ^ 1) for i in range(devices)]
    cross_route = [(i, (i + 1) % devices if i % 2 else (i - 1) % devices) for i in range(devices)]

    def across(block):
        return lax.ppermute(block, "docs", cross_route)

    order, bounds = slot_order(
        block_word, block_docs, block_count[0], position, own_blocks, devices
    )
    half_a, half_b, order, bounds = lax.optimization_barrier(
        (word_factor[:half], word_factor[half:], order, bounds)
    )
    cross_a = across(half_a)
    cross_b = across(half_b)
    partner = lax.ppermute(word_factor, "docs", partner_route)
    run = functools.partial(slots, order=order, bounds=bounds, counts=block_count_values, docs=doc_factor)
    grad_own, grad_h = run("own", words=word_factor, groups=(0, 8), base=0, do_w=True, do_h=True)
    grad_partner, grad_h = run(
        "partner", words=partner, groups=(8, 16), base=0, do_w=True, do_h=True, grad_h=grad_h
    )
    order_a, grad_partner = lax.optimization_barrier((order, grad_partner))
    (grad_a,) = run(
        "cross_a", order=order_a, words=cross_a, groups=(16, 20), base=0, do_w=True, do_h=False
    )
    order_b, sent_a = lax.optimization_barrier((order_a, grad_a.astype(jnp.float16)))
    from_a = across(sent_a)
    (grad_b,) = run(
        "cross_b", order=order_b, words=cross_b, groups=(20, 24), base=half_blocks, do_w=True, do_h=False
    )
    order_c, sent_b, grad_partner = lax.optimization_barrier(
        (order_b, grad_b.astype(jnp.float16), grad_partner)
    )
    from_b = across(sent_b)
    from_partner = lax.ppermute(grad_partner, "docs", partner_route)
    (grad_h,) = run(
        "late_a", order=order_c, words=cross_a, groups=(16, 20), base=0, do_w=False, do_h=True, grad_h=grad_h
    )
    (grad_h,) = run(
        "late_b", order=order_c, words=cross_b, groups=(20, 24), base=half_blocks, do_w=False, do_h=True, grad_h=grad_h
    )
    kept = grad_own + from_partner
    word_gradient = kept.at[:half].add(from_a.astype(F32)).at[half:].add(from_b.astype(F32))
    return (word_gradient, grad_h)


def solution(mesh):
    placed = (
        P("docs", None, None),
        P("docs", None),
        P(None, "docs"),
        P("docs"),
        P("docs"),
        P("docs"),
    )
    return jax.shard_map(
        on_device,
        mesh=mesh,
        in_specs=placed,
        out_specs=(P("docs", None), P(None, "docs")),
        check_vma=False,
    )
```

```python
import functools

import jax
import jax.numpy as jnp
from jax import lax
from jax.experimental import pallas as pl
from jax.experimental.pallas import tpu as pltpu
from jax.sharding import PartitionSpec as P

F32 = jnp.float32
BF16 = jnp.bfloat16
VMEM = pl.BlockSpec(memory_space=pltpu.VMEM)
SMEM = pl.BlockSpec(memory_space=pltpu.SMEM)
HBM = pl.BlockSpec(memory_space=pltpu.HBM)
DEAD = 1 << 10
RING = 8


def slot_kernel(spec, order, bounds, counts, words, docs, *refs):
    edge, first_group, last_group, base, do_w, do_h, carried = spec
    refs = list(refs)
    grad_h_in = refs.pop(0) if carried else None
    grad_w = refs.pop(0) if do_w else None
    grad_h = refs.pop(0) if do_h else None
    held, sems = refs
    first, last = bounds[first_group], bounds[last_group]

    def fetch(place):
        slot = order[place] & 63
        spot = (place - first) & (RING - 1)
        return pltpu.make_async_copy(counts.at[slot], held.at[spot], sems.at[spot])

    def fetched(place):
        return held[(place - first) & (RING - 1)].astype(F32)

    @pl.loop(first, jnp.minimum(first + RING - 2, last))
    def _(place):
        fetch(place).start()

    if do_w:
        grad_w[...] = jnp.zeros_like(grad_w)
    if do_h:
        grad_h[...] = grad_h_in[...] if carried else jnp.zeros_like(grad_h)

    def where_is(place):
        code = order[place]
        word = ((code >> 6) & 15) - base
        doc = code >> 10
        return (
            pl.ds(pl.multiple_of(word * edge, edge), edge),
            pl.ds(pl.multiple_of(doc * edge, edge), edge),
        )

    def product(rows, cols):
        return jnp.dot(words[rows, :], docs[:, cols], preferred_element_type=F32)

    def term_w(excess, cols):
        return lax.dot_general(
            excess, docs[:, cols], (((1,), (1,)), ((), ())), preferred_element_type=F32
        )

    def term_h(excess, rows):
        return lax.dot_general(
            words[rows, :], excess, (((0,), (0,)), ((), ())), preferred_element_type=F32
        )

    @pl.loop(0, (last - first + 1) // 2)
    def _(pair):
        one = first + 2 * pair
        two = jnp.minimum(one + 1, last - 1)
        paired = one + 1 < last

        @pl.loop(one + RING - 2, jnp.minimum(one + RING, last))
        def _(place):
            fetch(place).start()

        fetch(one).wait()

        @pl.when(paired)
        def _():
            fetch(two).wait()

        rows_one, cols_one = where_is(one)
        rows_two, cols_two = where_is(two)
        product_one = product(rows_one, cols_one)
        product_two = product(rows_two, cols_two)
        excess_one = (1.0 - fetched(one) / product_one).astype(BF16)
        excess_two = jnp.where(paired, 1.0 - fetched(two) / product_two, 0.0).astype(BF16)
        if do_w:
            term_w_one = term_w(excess_one, cols_one)
            term_w_two = term_w(excess_two, cols_two)
        if do_h:
            term_h_one = term_h(excess_one, rows_one)
            term_h_two = term_h(excess_two, rows_two)
        if do_w:
            grad_w[rows_one, :] += term_w_one
            grad_w[rows_two, :] += term_w_two
        if do_h:
            grad_h[:, cols_one] += term_h_one
            grad_h[:, cols_two] += term_h_two


def slots(name, order, bounds, counts, words, docs, groups, base, do_w, do_h, grad_h=None, flops=1):
    edge = counts.shape[1]
    carried = grad_h is not None
    spec = (edge, groups[0], groups[1], base, do_w, do_h, carried)
    operands = [order, bounds, counts, words, docs] + ([grad_h] if carried else [])
    shapes = []
    if do_w:
        shapes.append(jax.ShapeDtypeStruct(words.shape, F32))
    if do_h:
        shapes.append(jax.ShapeDtypeStruct(docs.shape, F32))
    return pl.pallas_call(
        functools.partial(slot_kernel, spec),
        out_shape=shapes,
        in_specs=[SMEM, SMEM, HBM, VMEM, VMEM] + ([VMEM] if carried else []),
        out_specs=[VMEM] * len(shapes),
        scratch_shapes=[
            pltpu.VMEM((RING,) + counts.shape[1:], counts.dtype),
            pltpu.SemaphoreType.DMA((RING,)),
        ],
        input_output_aliases={5: int(do_w)} if carried else {},
        compiler_params=pltpu.CompilerParams(vmem_limit_bytes=20 << 20),
        cost_estimate=pl.CostEstimate(flops=flops, bytes_accessed=1, transcendentals=0),
        name=name,
    )(*operands)


def slot_order(block_word, block_docs, live, position, own_blocks, devices):
    slot = jnp.arange(block_word.shape[0], dtype=jnp.int32)
    local = jnp.mod(block_word - (position - 1) * own_blocks, own_blocks * devices)
    side = local // own_blocks
    inner = local - side * own_blocks
    even = position % 2 == 0
    group = jnp.where(side == 1, 0, jnp.where((side == 0) == even, 2, 1))
    key = jnp.where(slot < live, group * own_blocks + inner, DEAD)
    rank_key = key * 64 + slot
    rank = jnp.sum((rank_key[None, :] < rank_key[:, None]).astype(jnp.int32), axis=1)
    code = slot + inner * 64 + block_docs * 1024
    order = jnp.sum(jnp.where(rank[:, None] == slot[None, :], code[:, None], 0), axis=0)
    marks = jnp.arange(3 * own_blocks + 1, dtype=jnp.int32)
    bounds = jnp.sum((key[None, :] < marks[:, None]).astype(jnp.int32), axis=1)
    return order, bounds


def on_device(block_count_values, word_factor, doc_factor, block_word, block_docs, block_count):
    devices = lax.axis_size("docs")
    position = lax.axis_index("docs")
    edge = block_count_values.shape[1]
    rows = word_factor.shape[0]
    own_blocks = rows // edge
    split = own_blocks // 2
    half = split * edge
    side = (0, own_blocks, 2 * own_blocks, 2 * own_blocks + split, 3 * own_blocks)
    partner_route = [(i, i ^ 1) for i in range(devices)]
    cross_route = [(i, (i + 1) % devices if i % 2 else (i - 1) % devices) for i in range(devices)]

    def across(block):
        return lax.ppermute(block, "docs", cross_route)

    half_a, word_factor = lax.optimization_barrier((word_factor[:half], word_factor))
    half_b, half_a, word_factor = lax.optimization_barrier((word_factor[half:], half_a, word_factor))
    cross_a = across(half_a)
    cross_b = across(half_b)
    partner = lax.ppermute(word_factor, "docs", partner_route)
    order, bounds = slot_order(
        block_word, block_docs, block_count[0], position, own_blocks, devices
    )
    order, half_b = lax.optimization_barrier((order, half_b))
    run = functools.partial(slots, bounds=bounds, counts=pltpu.with_memory_space_constraint(block_count_values, pltpu.HBM), docs=doc_factor)
    grad_own, grad_h = run(
        "own", order=order, words=word_factor, groups=side[0:2], base=0, do_w=True, do_h=True
    )
    grad_partner, grad_h = run(
        "partner", order=order, words=partner, groups=side[1:3], base=0, do_w=True, do_h=True, grad_h=grad_h
    )
    order, grad_partner = lax.optimization_barrier((order, grad_partner))
    (grad_a,) = run(
        "cross_a", order=order, words=cross_a, groups=side[2:4], base=0, do_w=True, do_h=False
    )
    order, sent_a = lax.optimization_barrier((order, grad_a.astype(jnp.float16)))
    from_a = across(sent_a)
    (grad_h,) = run(
        "late_a", order=order, words=cross_a, groups=side[2:4], base=0, do_w=False, do_h=True, grad_h=grad_h
    )
    order, grad_h = lax.optimization_barrier((order, grad_h))
    (grad_b,) = run(
        "cross_b", order=order, words=cross_b, groups=side[3:5], base=split, do_w=True, do_h=False
    )
    order, sent_b, from_a, grad_partner = lax.optimization_barrier(
        (order, grad_b.astype(jnp.float16), from_a, grad_partner)
    )
    from_b = across(sent_b)
    from_partner = lax.ppermute(grad_partner, "docs", partner_route)
    sum_a = grad_own[:half] + from_a.astype(F32)
    order, sum_a = lax.optimization_barrier((order, sum_a))
    (grad_h,) = run(
        "late_b", order=order, words=cross_b, groups=side[3:5], base=split, do_w=False, do_h=True, grad_h=grad_h
    )
    grad_h, from_partner = lax.optimization_barrier((grad_h, from_partner))
    sum_a = sum_a + from_partner[:half]
    kept_b = grad_own[half:] + from_partner[half:]
    kept_b, sum_a = lax.optimization_barrier((kept_b, sum_a))
    word_gradient = jnp.concatenate([sum_a, kept_b + from_b.astype(F32)])
    return (word_gradient, grad_h)


def solution(mesh):
    placed = (
        P("docs", None, None),
        P("docs", None),
        P(None, "docs"),
        P("docs"),
        P("docs"),
        P("docs"),
    )
    return jax.shard_map(
        on_device,
        mesh=mesh,
        in_specs=placed,
        out_specs=(P("docs", None), P(None, "docs")),
        check_vma=False,
    )
```

```python
import functools

import jax
import jax.numpy as jnp
from jax import lax
from jax.experimental import pallas as pl
from jax.experimental.pallas import tpu as pltpu
from jax.sharding import PartitionSpec as P

F32 = jnp.float32
BF16 = jnp.bfloat16
F16 = jnp.float16
VMEM = pl.BlockSpec(memory_space=pltpu.VMEM)
SMEM = pl.BlockSpec(memory_space=pltpu.SMEM)
HBM = pl.BlockSpec(memory_space=pltpu.HBM)
DEAD = 1 << 10
GROUP = 4
RING = 2 * GROUP
CHEAP = pl.CostEstimate(flops=1, bytes_accessed=1, transcendentals=0)


def params(megabytes):
    return pltpu.CompilerParams(vmem_limit_bytes=megabytes << 20)


def block_at(index, edge):
    return pl.ds(pl.multiple_of(index * edge, edge), edge)


def code_parts(code):
    return code & 63, (code >> 6) & 15, code >> 10


def halves_kernel(split, source, low, high, sems):
    copies = [
        pltpu.make_async_copy(source.at[pl.ds(0, split)], low, sems.at[0]),
        pltpu.make_async_copy(
            source.at[pl.ds(split, source.shape[0] - split)], high, sems.at[1]
        ),
    ]
    for copy in copies:
        copy.start()
    for copy in copies:
        copy.wait()


def halves(block, split):
    rows, width = block.shape
    return pl.pallas_call(
        functools.partial(halves_kernel, split),
        out_shape=[
            jax.ShapeDtypeStruct((split, width), block.dtype),
            jax.ShapeDtypeStruct((rows - split, width), block.dtype),
        ],
        in_specs=[HBM],
        out_specs=[HBM, HBM],
        scratch_shapes=[pltpu.SemaphoreType.DMA((2,))],
        cost_estimate=CHEAP,
        name="halves",
    )(block)


def word_kernel(spec, order, bounds, counts, words, docs, *refs):
    edge, first_mark, last_mark, base, chained = spec
    if chained:
        refs = refs[1:]
    grad, kept, held, staged, sems, out_sems = refs
    first, last = bounds[first_mark], bounds[last_mark]

    def fetch(place):
        slot, _, _ = code_parts(order[place])
        spot = (place - first) & (RING - 1)
        return pltpu.make_async_copy(counts.at[slot], held.at[spot], sems.at[spot])

    def keep(place, spot):
        return pltpu.make_async_copy(staged.at[spot], kept.at[place], out_sems.at[spot])

    @pl.loop(first, jnp.minimum(first + GROUP, last))
    def _(place):
        fetch(place).start()

    grad[...] = jnp.zeros_like(grad)

    @pl.loop(0, (last - first + GROUP - 1) // GROUP)
    def _(step):
        start = first + GROUP * step

        @pl.loop(start + GROUP, jnp.minimum(start + 2 * GROUP, last))
        def _(place):
            fetch(place).start()

        @pl.loop(start, jnp.minimum(start + GROUP, last))
        def _(place):
            fetch(place).wait()

        half = (step & 1) * GROUP

        @pl.when(step > 1)
        def _():
            for g in range(GROUP):
                keep(start + g - 2 * GROUP, half + g).wait()

        places = [jnp.minimum(start + g, last - 1) for g in range(GROUP)]
        parts = [code_parts(order[place]) for place in places]
        rows = [block_at(word - base, edge) for _, word, _ in parts]
        cols = [block_at(doc, edge) for _, _, doc in parts]
        products = [
            jnp.dot(words[r, :], docs[:, c], preferred_element_type=F32) for r, c in zip(rows, cols)
        ]
        excess = []
        for g in range(GROUP):
            ratio = held[(places[g] - first) & (RING - 1)].astype(F32) / products[g]
            one = (1.0 - ratio).astype(BF16)
            if g:
                one = jnp.where(start + g < last, one, jnp.zeros_like(one))
            excess.append(one)
            staged[half + g] = one
        terms = [
            lax.dot_general(e, docs[:, c], (((1,), (1,)), ((), ())), preferred_element_type=F32)
            for e, c in zip(excess, cols)
        ]
        for g in range(GROUP):
            grad[rows[g], :] += terms[g]

        @pl.loop(start, jnp.minimum(start + GROUP, last))
        def _(place):
            keep(place, half + place - start).start()

    steps = (last - first + GROUP - 1) // GROUP

    @pl.loop(first + GROUP * jnp.maximum(steps - 2, 0), last)
    def _(place):
        keep(place, (place - first) & (RING - 1)).wait()


def word_terms(name, order, bounds, counts, words, docs, marks, base, kept=None):
    slots, edge, _ = counts.shape
    chained = kept is not None
    spec = (edge, marks[0], marks[1], base, chained)
    return pl.pallas_call(
        functools.partial(word_kernel, spec),
        out_shape=[
            jax.ShapeDtypeStruct(words.shape, F32),
            jax.ShapeDtypeStruct((slots, edge, edge), BF16),
        ],
        in_specs=[SMEM, SMEM, HBM, VMEM, VMEM] + [HBM] * chained,
        out_specs=[VMEM, HBM],
        scratch_shapes=[
            pltpu.VMEM((RING, edge, edge), counts.dtype),
            pltpu.VMEM((RING, edge, edge), BF16),
            pltpu.SemaphoreType.DMA((RING,)),
            pltpu.SemaphoreType.DMA((RING,)),
        ],
        input_output_aliases={5: 1} if chained else {},
        compiler_params=params(16),
        cost_estimate=CHEAP,
        name=name,
    )(order, bounds, counts, words, docs, *([kept] if chained else []))


def doc_kernel(spec, order, bounds, kept, *refs):
    edge, marks, bases = spec
    sides, grad, held, sems = refs[: len(bases)], refs[-3], refs[-2], refs[-1]
    total = bounds[marks[-1]]

    def fetch(place):
        spot = place & (RING - 1)
        return pltpu.make_async_copy(kept.at[place], held.at[spot], sems.at[spot])

    @pl.loop(0, jnp.minimum(GROUP, total))
    def _(place):
        fetch(place).start()

    grad[...] = jnp.zeros_like(grad)
    for words, base, first_mark, last_mark in zip(sides, bases, marks, marks[1:]):
        first, last = bounds[first_mark], bounds[last_mark]

        @pl.loop(0, (last - first + 1) // 2)
        def _(step, words=words, base=base, first=first, last=last):
            start = first + 2 * step

            @pl.loop(start, jnp.minimum(start + 2, last))
            def _(place):
                @pl.when(place + GROUP < total)
                def _():
                    fetch(place + GROUP).start()

                fetch(place).wait()

            places = [start, jnp.minimum(start + 1, last - 1)]
            parts = [code_parts(order[place]) for place in places]
            cols = [block_at(doc, edge) for _, _, doc in parts]
            one = held[places[0] & (RING - 1)]
            two = held[places[1] & (RING - 1)]
            two = jnp.where(start + 1 < last, two, jnp.zeros_like(two))
            terms = [
                lax.dot_general(
                    words[block_at(word - base, edge), :],
                    e,
                    (((0,), (0,)), ((), ())),
                    preferred_element_type=F32,
                )
                for (_, word, _), e in zip(parts, (one, two))
            ]
            for c, term in zip(cols, terms):
                grad[:, c] += term


def doc_terms(order, bounds, kept, sides, marks, bases, width):
    slots, edge, _ = kept.shape
    rank = sides[0].shape[1]
    return pl.pallas_call(
        functools.partial(doc_kernel, (edge, marks, bases)),
        out_shape=jax.ShapeDtypeStruct((rank, width), F32),
        in_specs=[SMEM, SMEM, HBM] + [VMEM] * len(sides),
        out_specs=VMEM,
        scratch_shapes=[pltpu.VMEM((RING, edge, edge), BF16), pltpu.SemaphoreType.DMA((RING,))],
        compiler_params=params(16),
        cost_estimate=CHEAP,
        name="docs",
    )(order, bounds, kept, *sides)


def finish_kernel(start, pieces, chained, *refs):
    own, near, far = refs[:3]
    out, sums, sems = refs[-3:]
    rows = far.shape[0] // pieces
    copies = []
    for piece in range(pieces):
        here = pl.ds(piece * rows, rows)
        there = pl.ds(start + piece * rows, rows)
        sums[here, :] = own[there, :] + near[there, :] + far[here, :]
        copies.append(pltpu.make_async_copy(sums.at[here], out.at[there], sems.at[piece]))
        copies[-1].start()
    for copy in copies:
        copy.wait()


def finish(name, own, near, far, start, result=None):
    chained = result is not None
    pieces = 4
    return pl.pallas_call(
        functools.partial(finish_kernel, start, pieces, chained),
        out_shape=jax.ShapeDtypeStruct(own.shape, F32),
        in_specs=[VMEM] * 3 + [HBM] * chained,
        out_specs=HBM,
        scratch_shapes=[pltpu.VMEM(far.shape, F32), pltpu.SemaphoreType.DMA((pieces,))],
        input_output_aliases={3: 0} if chained else {},
        compiler_params=params(16),
        cost_estimate=CHEAP,
        name=name,
    )(own, near, far, *([result] if chained else []))


def slot_order(block_word, block_docs, live, position, own_blocks, devices):
    slot = jnp.arange(block_word.shape[0], dtype=jnp.int32)
    local = jnp.mod(block_word - (position - 1) * own_blocks, own_blocks * devices)
    side = local // own_blocks
    inner = local - side * own_blocks
    even = position % 2 == 0
    group = jnp.where(side == 1, 0, jnp.where((side == 0) == even, 2, 1))
    key = jnp.where(slot < live, group * own_blocks + inner, DEAD)
    rank_key = key * 64 + slot
    rank = jnp.sum((rank_key[None, :] < rank_key[:, None]).astype(jnp.int32), axis=1)
    code = slot + inner * 64 + block_docs * 1024
    order = jnp.sum(jnp.where(rank[:, None] == slot[None, :], code[:, None], 0), axis=0)
    marks = jnp.arange(3 * own_blocks + 1, dtype=jnp.int32)
    bounds = jnp.sum((key[None, :] < marks[:, None]).astype(jnp.int32), axis=1)
    return order, bounds


def on_device(block_count_values, word_factor, doc_factor, block_word, block_docs, block_count):
    devices = lax.axis_size("docs")
    position = lax.axis_index("docs")
    edge = block_count_values.shape[1]
    rows = word_factor.shape[0]
    own_blocks = rows // edge
    split = own_blocks // 2
    half = split * edge
    marks = (0, own_blocks, 2 * own_blocks, 2 * own_blocks + split, 3 * own_blocks)
    partner_route = [(i, i ^ 1) for i in range(devices)]
    cross_route = [(i, (i + 1) % devices if i % 2 else (i - 1) % devices) for i in range(devices)]

    def across(block):
        return lax.ppermute(block, "docs", cross_route)

    half_a, half_b = halves(word_factor, half)
    cross_a = across(half_a)
    cross_b = across(half_b)
    half_b, word_factor = lax.optimization_barrier((half_b, word_factor))
    partner = lax.ppermute(word_factor, "docs", partner_route)
    order, bounds = slot_order(
        block_word, block_docs, block_count[0], position, own_blocks, devices
    )
    order, half_b = lax.optimization_barrier((order, half_b))
    counts = pltpu.with_memory_space_constraint(block_count_values, pltpu.HBM)
    run = functools.partial(word_terms, bounds=bounds, counts=counts, docs=doc_factor)
    own, kept = run("own", order=order, words=word_factor, marks=marks[0:2], base=0)
    near, kept = run("partner", order=order, words=partner, marks=marks[1:3], base=0, kept=kept)
    order, near = lax.optimization_barrier((order, near))
    far_a, kept = run("cross_a", order=order, words=cross_a, marks=marks[2:4], base=0, kept=kept)
    order, far_a = lax.optimization_barrier((order, far_a.astype(F16)))
    far_a = across(far_a)
    far_b, kept = run("cross_b", order=order, words=cross_b, marks=marks[3:5], base=split, kept=kept)
    order, far_b, far_a, near = lax.optimization_barrier((order, far_b.astype(F16), far_a, near))
    far_b = across(far_b)
    near = lax.ppermute(near, "docs", partner_route)
    document_gradient = doc_terms(
        order,
        bounds,
        kept,
        (word_factor, partner, cross_a, cross_b),
        marks,
        (0, 0, 0, split),
        doc_factor.shape[1],
    )
    document_gradient, near = lax.optimization_barrier((document_gradient, near))
    result = finish("finish_a", own, near, far_a.astype(F32), 0)
    result, far_b = lax.optimization_barrier((result, far_b))
    result = finish("finish_b", own, near, far_b.astype(F32), half, result)
    return (result, document_gradient)


def solution(mesh):
    placed = (
        P("docs", None, None),
        P("docs", None),
        P(None, "docs"),
        P("docs"),
        P("docs"),
        P("docs"),
    )
    return jax.shard_map(
        on_device,
        mesh=mesh,
        in_specs=placed,
        out_specs=(P("docs", None), P(None, "docs")),
        check_vma=False,
    )
```

```python
import functools

import jax
import jax.numpy as jnp
from jax import lax
from jax.experimental import pallas as pl
from jax.experimental.pallas import tpu as pltpu
from jax.sharding import PartitionSpec as P

F32 = jnp.float32
BF16 = jnp.bfloat16
F16 = jnp.float16
VMEM = pl.BlockSpec(memory_space=pltpu.VMEM)
SMEM = pl.BlockSpec(memory_space=pltpu.SMEM)
HBM = pl.BlockSpec(memory_space=pltpu.HBM)
DEAD = 1 << 10
GROUP = 4
RING = 2 * GROUP
CHEAP = pl.CostEstimate(flops=1, bytes_accessed=1, transcendentals=0)


def params(megabytes):
    return pltpu.CompilerParams(vmem_limit_bytes=megabytes << 20)


def block_at(index, edge):
    return pl.ds(pl.multiple_of(index * edge, edge), edge)


def code_parts(code):
    return code & 63, (code >> 6) & 15, code >> 10


def word_kernel(spec, order, bounds, counts, words, docs, *refs):
    edge, first_mark, last_mark, base, chained = spec
    if chained:
        refs = refs[1:]
    grad, kept, held, staged, sems, out_sems = refs
    first, last = bounds[first_mark], bounds[last_mark]

    def fetch(place):
        slot, _, _ = code_parts(order[place])
        return pltpu.make_async_copy(counts.at[slot], held.at[place], sems.at[place])

    def keep(place, spot):
        return pltpu.make_async_copy(staged.at[spot], kept.at[place], out_sems.at[spot])

    @pl.loop(first, last)
    def _(place):
        fetch(place).start()

    grad[...] = jnp.zeros_like(grad)

    @pl.loop(0, (last - first + GROUP - 1) // GROUP)
    def _(step):
        start = first + GROUP * step

        @pl.loop(start, jnp.minimum(start + GROUP, last))
        def _(place):
            fetch(place).wait()

        half = (step & 1) * GROUP

        @pl.when(step > 1)
        def _():
            for g in range(GROUP):
                keep(start + g - 2 * GROUP, half + g).wait()

        places = [jnp.minimum(start + g, last - 1) for g in range(GROUP)]
        parts = [code_parts(order[place]) for place in places]
        rows = [block_at(word, edge) for _, word, _ in parts]
        sums = [block_at(word - base, edge) for _, word, _ in parts]
        cols = [block_at(doc, edge) for _, _, doc in parts]
        products = [
            jnp.dot(words[r, :], docs[:, c], preferred_element_type=F32) for r, c in zip(rows, cols)
        ]
        excess = []
        for g in range(GROUP):
            ratio = held[places[g]].astype(F32) / products[g]
            one = (1.0 - ratio).astype(BF16)
            if g:
                one = jnp.where(start + g < last, one, jnp.zeros_like(one))
            excess.append(one)
            staged[half + g] = one
        terms = [
            lax.dot_general(e, docs[:, c], (((1,), (1,)), ((), ())), preferred_element_type=F32)
            for e, c in zip(excess, cols)
        ]
        for g in range(GROUP):
            grad[sums[g], :] += terms[g]

        @pl.loop(start, jnp.minimum(start + GROUP, last))
        def _(place):
            keep(place, half + place - start).start()

    steps = (last - first + GROUP - 1) // GROUP

    @pl.loop(first + GROUP * jnp.maximum(steps - 2, 0), last)
    def _(place):
        keep(place, (place - first) & (RING - 1)).wait()


def word_terms(name, order, bounds, counts, words, docs, marks, part=None, kept=None):
    slots, edge, _ = counts.shape
    chained = kept is not None
    low, high = part or (0, words.shape[0] // edge)
    spec = (edge, marks[0], marks[1], low, chained)
    return pl.pallas_call(
        functools.partial(word_kernel, spec),
        out_shape=[
            jax.ShapeDtypeStruct(((high - low) * edge, words.shape[1]), F32),
            jax.ShapeDtypeStruct((slots, edge, edge), BF16),
        ],
        in_specs=[SMEM, SMEM, HBM, VMEM, VMEM] + [HBM] * chained,
        out_specs=[VMEM, HBM],
        scratch_shapes=[
            pltpu.VMEM((slots, edge, edge), counts.dtype),
            pltpu.VMEM((RING, edge, edge), BF16),
            pltpu.SemaphoreType.DMA((slots,)),
            pltpu.SemaphoreType.DMA((RING,)),
        ],
        input_output_aliases={5: 1} if chained else {},
        compiler_params=params(20),
        cost_estimate=CHEAP,
        name=name,
    )(order, bounds, counts, words, docs, *([kept] if chained else []))


def doc_kernel(spec, order, bounds, kept, *refs):
    edge, marks = spec
    sides, grad, held, sems = refs[:-3], refs[-3], refs[-2], refs[-1]
    total = bounds[marks[-1]]

    def fetch(place):
        return pltpu.make_async_copy(kept.at[place], held.at[place], sems.at[place])

    @pl.loop(0, total)
    def _(place):
        fetch(place).start()

    grad[...] = jnp.zeros_like(grad)
    for words, first_mark, last_mark in zip(sides, marks, marks[1:]):
        first, last = bounds[first_mark], bounds[last_mark]

        @pl.loop(0, (last - first + GROUP - 1) // GROUP)
        def _(step, words=words, first=first, last=last):
            start = first + GROUP * step

            @pl.loop(start, jnp.minimum(start + GROUP, last))
            def _(place):
                fetch(place).wait()

            places = [jnp.minimum(start + g, last - 1) for g in range(GROUP)]
            parts = [code_parts(order[place]) for place in places]
            cols = [block_at(doc, edge) for _, _, doc in parts]
            terms = []
            for g in range(GROUP):
                one = held[places[g]]
                if g:
                    one = jnp.where(start + g < last, one, jnp.zeros_like(one))
                rows = block_at(parts[g][1], edge)
                terms.append(
                    lax.dot_general(
                        words[rows, :], one, (((0,), (0,)), ((), ())), preferred_element_type=F32
                    )
                )
            for c, term in zip(cols, terms):
                grad[:, c] += term


def doc_terms(order, bounds, kept, sides, marks, width):
    slots, edge, _ = kept.shape
    rank = sides[0].shape[1]
    return pl.pallas_call(
        functools.partial(doc_kernel, (edge, marks)),
        out_shape=jax.ShapeDtypeStruct((rank, width), F32),
        in_specs=[SMEM, SMEM, HBM] + [VMEM] * len(sides),
        out_specs=VMEM,
        scratch_shapes=[pltpu.VMEM((slots, edge, edge), BF16), pltpu.SemaphoreType.DMA((slots,))],
        compiler_params=params(16),
        cost_estimate=CHEAP,
        name="docs",
    )(order, bounds, kept, *sides)


def finish_kernel(start, pieces, chained, *refs):
    own, near, far = refs[:3]
    out, sums, sems = refs[-3:]
    rows = far.shape[0] // pieces
    copies = []
    for piece in range(pieces):
        here = pl.ds(piece * rows, rows)
        there = pl.ds(start + piece * rows, rows)
        sums[here, :] = own[there, :] + near[there, :] + far[here, :]
        copies.append(pltpu.make_async_copy(sums.at[here], out.at[there], sems.at[piece]))
        copies[-1].start()
    for copy in copies:
        copy.wait()


def finish(name, own, near, far, start, result=None):
    chained = result is not None
    pieces = 4
    return pl.pallas_call(
        functools.partial(finish_kernel, start, pieces, chained),
        out_shape=jax.ShapeDtypeStruct(own.shape, F32),
        in_specs=[VMEM] * 3 + [HBM] * chained,
        out_specs=HBM,
        scratch_shapes=[pltpu.VMEM(far.shape, F32), pltpu.SemaphoreType.DMA((pieces,))],
        input_output_aliases={3: 0} if chained else {},
        compiler_params=params(16),
        cost_estimate=CHEAP,
        name=name,
    )(own, near, far, *([result] if chained else []))


def slot_order(block_word, block_docs, live, position, own_blocks, devices):
    slot = jnp.arange(block_word.shape[0], dtype=jnp.int32)
    local = jnp.mod(block_word - (position - 1) * own_blocks, own_blocks * devices)
    side = local // own_blocks
    inner = local - side * own_blocks
    even = position % 2 == 0
    group = jnp.where(side == 1, 0, jnp.where((side == 0) == even, 2, 1))
    key = jnp.where(slot < live, group * own_blocks + inner, DEAD)
    rank_key = key * 64 + slot
    rank = jnp.sum((rank_key[None, :] < rank_key[:, None]).astype(jnp.int32), axis=1)
    code = slot + inner * 64 + block_docs * 1024
    order = jnp.sum(jnp.where(rank[:, None] == slot[None, :], code[:, None], 0), axis=0)
    marks = jnp.arange(3 * own_blocks + 1, dtype=jnp.int32)
    bounds = jnp.sum((key[None, :] < marks[:, None]).astype(jnp.int32), axis=1)
    return order, bounds


def on_device(block_count_values, word_factor, doc_factor, block_word, block_docs, block_count):
    devices = lax.axis_size("docs")
    position = lax.axis_index("docs")
    edge = block_count_values.shape[1]
    rows = word_factor.shape[0]
    own_blocks = rows // edge
    split = own_blocks // 2
    half = split * edge
    marks = (0, own_blocks, 2 * own_blocks, 2 * own_blocks + split, 3 * own_blocks)
    partner_route = [(i, i ^ 1) for i in range(devices)]
    cross_route = [(i, (i + 1) % devices if i % 2 else (i - 1) % devices) for i in range(devices)]

    def across(block):
        return lax.ppermute(block, "docs", cross_route)

    there = across(word_factor)
    partner = lax.ppermute(word_factor, "docs", partner_route)
    order, bounds = slot_order(
        block_word, block_docs, block_count[0], position, own_blocks, devices
    )
    counts = pltpu.with_memory_space_constraint(block_count_values, pltpu.HBM)
    run = functools.partial(word_terms, bounds=bounds, counts=counts, docs=doc_factor)
    own, kept = run("own", order=order, words=word_factor, marks=marks[0:2])
    near, kept = run("partner", order=order, words=partner, marks=marks[1:3], kept=kept)
    order, near = lax.optimization_barrier((order, near))
    near = lax.ppermute(near, "docs", partner_route)
    far_a, kept = run("cross_a", order=order, words=there, marks=marks[2:4], kept=kept, part=(0, split))
    order, far_a = lax.optimization_barrier((order, far_a.astype(F16)))
    far_a = across(far_a)
    far_b, kept = run(
        "cross_b", order=order, words=there, marks=marks[3:5], kept=kept, part=(split, own_blocks)
    )
    order, far_b, far_a = lax.optimization_barrier((order, far_b.astype(F16), far_a))
    far_b = across(far_b)
    document_gradient = doc_terms(
        order,
        bounds,
        kept,
        (word_factor, partner, there),
        (0, own_blocks, 2 * own_blocks, 3 * own_blocks),
        doc_factor.shape[1],
    )
    document_gradient, near = lax.optimization_barrier((document_gradient, near))
    result = finish("finish_a", own, near, far_a.astype(F32), 0)
    result, far_b = lax.optimization_barrier((result, far_b))
    result = finish("finish_b", own, near, far_b.astype(F32), half, result)
    return (result, document_gradient)


def solution(mesh):
    placed = (
        P("docs", None, None),
        P("docs", None),
        P(None, "docs"),
        P("docs"),
        P("docs"),
        P("docs"),
    )
    return jax.shard_map(
        on_device,
        mesh=mesh,
        in_specs=placed,
        out_specs=(P("docs", None), P(None, "docs")),
        check_vma=False,
    )
```

```python
import functools

import jax
import jax.numpy as jnp
from jax import lax
from jax.experimental import pallas as pl
from jax.experimental.pallas import tpu as pltpu
from jax.sharding import PartitionSpec as P

F32 = jnp.float32
BF16 = jnp.bfloat16
F16 = jnp.float16
VMEM = pl.BlockSpec(memory_space=pltpu.VMEM)
SMEM = pl.BlockSpec(memory_space=pltpu.SMEM)
HBM = pl.BlockSpec(memory_space=pltpu.HBM)
DEAD = 1 << 10
GROUP = 4
RING = 2 * GROUP
CHEAP = pl.CostEstimate(flops=1, bytes_accessed=1, transcendentals=0)


def params(megabytes):
    return pltpu.CompilerParams(vmem_limit_bytes=megabytes << 20)


def block_at(index, edge):
    return pl.ds(pl.multiple_of(index * edge, edge), edge)


def code_parts(code):
    return code & 63, (code >> 6) & 15, code >> 10


def word_kernel(spec, order, bounds, counts, words, docs, *refs):
    edge, first_mark, last_mark, base, chained = spec
    if chained:
        refs = refs[1:]
    grad, kept, held, staged, sems, out_sems = refs
    first, last = bounds[first_mark], bounds[last_mark]

    top = order.shape[0] - 1
    steps = (last - first + GROUP - 1) // GROUP

    def fetch(place):
        slot, _, _ = code_parts(order[jnp.minimum(place, top)])
        return pltpu.make_async_copy(counts.at[slot], held.at[place], sems.at[place])

    def keep(place, spot):
        return pltpu.make_async_copy(staged.at[spot], kept.at[place], out_sems.at[spot])

    @pl.loop(first, first + steps * GROUP)
    def _(place):
        fetch(place).start()

    grad[...] = jnp.zeros_like(grad)

    @pl.loop(0, steps)
    def _(step):
        start = first + GROUP * step
        half = (step & 1) * GROUP
        for g in range(GROUP):
            fetch(start + g).wait()

        @pl.when(step > 1)
        def _():
            for g in range(GROUP):
                keep(start + g - 2 * GROUP, half + g).wait()

        parts = [code_parts(order[jnp.minimum(start + g, last - 1)]) for g in range(GROUP)]
        rows = [block_at(word, edge) for _, word, _ in parts]
        sums = [block_at(word - base, edge) for _, word, _ in parts]
        cols = [block_at(doc, edge) for _, _, doc in parts]
        products = [
            jnp.dot(words[r, :], docs[:, c], preferred_element_type=F32) for r, c in zip(rows, cols)
        ]
        excess = []
        for g in range(GROUP):
            ratio = held[start + g].astype(F32) / products[g]
            one = (1.0 - ratio).astype(BF16)
            if g:
                one = jnp.where(start + g < last, one, jnp.zeros_like(one))
            excess.append(one)
            staged[half + g] = one
        terms = [
            lax.dot_general(e, docs[:, c], (((1,), (1,)), ((), ())), preferred_element_type=F32)
            for e, c in zip(excess, cols)
        ]
        for g in range(GROUP):
            grad[sums[g], :] += terms[g]
        for g in range(GROUP):
            keep(start + g, half + g).start()

    @pl.loop(GROUP * jnp.maximum(steps - 2, 0), GROUP * steps)
    def _(place):
        keep(first + place, place & (RING - 1)).wait()


def word_terms(name, order, bounds, counts, words, docs, marks, part=None, kept=None):
    slots, edge, _ = counts.shape
    chained = kept is not None
    low, high = part or (0, words.shape[0] // edge)
    spec = (edge, marks[0], marks[1], low, chained)
    return pl.pallas_call(
        functools.partial(word_kernel, spec),
        out_shape=[
            jax.ShapeDtypeStruct(((high - low) * edge, words.shape[1]), F32),
            pltpu.HBM((slots + GROUP, edge, edge), BF16),
        ],
        in_specs=[SMEM, SMEM, HBM, VMEM, VMEM] + [HBM] * chained,
        out_specs=[VMEM, HBM],
        scratch_shapes=[
            pltpu.VMEM((slots + GROUP, edge, edge), counts.dtype),
            pltpu.VMEM((RING, edge, edge), BF16),
            pltpu.SemaphoreType.DMA((slots + GROUP,)),
            pltpu.SemaphoreType.DMA((RING,)),
        ],
        input_output_aliases={5: 1} if chained else {},
        compiler_params=params(20),
        cost_estimate=CHEAP,
        name=name,
    )(order, bounds, counts, words, docs, *([kept] if chained else []))


def doc_kernel(spec, order, bounds, kept, *refs):
    edge, marks = spec
    sides, (grad, words, held, side_sems, sems) = refs[:-5], refs[-5:]
    rows = sides[0].shape[0]
    blocks = rows // edge
    total = bounds[marks[-1]]
    steps = (total + GROUP - 1) // GROUP
    empty = kept.shape[0]
    loads = [
        pltpu.make_async_copy(side, words.at[pl.ds(i * rows, rows)], side_sems.at[i])
        for i, side in enumerate(sides)
    ]
    for load in loads:
        load.start()

    def fetch(place):
        return pltpu.make_async_copy(kept.at[place], held.at[place], sems.at[place])

    @pl.loop(0, steps * GROUP)
    def _(place):
        fetch(place).start()

    held[empty] = jnp.zeros(held.shape[1:], held.dtype)
    grad[...] = jnp.zeros_like(grad)
    for load in loads:
        load.wait()

    def side_of(place):
        return sum((place >= bounds[mark]).astype(jnp.int32) for mark in marks[1:-1])

    @pl.loop(0, steps)
    def _(step):
        start = GROUP * step
        for g in range(GROUP):
            fetch(start + g).wait()
        cols, terms = [], []
        for g in range(GROUP):
            place = jnp.minimum(start + g, total - 1)
            _, word, doc = code_parts(order[place])
            one = held[jnp.where(start + g < total, place, empty)]
            cols.append(block_at(doc, edge))
            terms.append(
                lax.dot_general(
                    words[block_at(word + side_of(place) * blocks, edge), :],
                    one,
                    (((0,), (0,)), ((), ())),
                    preferred_element_type=F32,
                )
            )
        for c, term in zip(cols, terms):
            grad[:, c] += term


def doc_terms(order, bounds, kept, sides, marks, width):
    spots, edge, _ = kept.shape
    rows, rank = sides[0].shape
    return pl.pallas_call(
        functools.partial(doc_kernel, (edge, marks)),
        out_shape=jax.ShapeDtypeStruct((rank, width), F32),
        in_specs=[SMEM, SMEM, HBM] + [pl.BlockSpec(memory_space=pl.ANY)] * len(sides),
        out_specs=VMEM,
        scratch_shapes=[
            pltpu.VMEM((len(sides) * rows, rank), BF16),
            pltpu.VMEM((spots + 1, edge, edge), BF16),
            pltpu.SemaphoreType.DMA((len(sides),)),
            pltpu.SemaphoreType.DMA((spots,)),
        ],
        compiler_params=params(20),
        cost_estimate=CHEAP,
        name="docs",
    )(order, bounds, pltpu.with_memory_space_constraint(kept, pltpu.HBM), *sides)


def finish_kernel(start, pieces, chained, *refs):
    own, near, far = refs[:3]
    out, sums, sems = refs[-3:]
    rows = far.shape[0] // pieces
    copies = []
    for piece in range(pieces):
        here = pl.ds(piece * rows, rows)
        there = pl.ds(start + piece * rows, rows)
        sums[here, :] = own[there, :] + near[there, :] + far[here, :]
        copies.append(pltpu.make_async_copy(sums.at[here], out.at[there], sems.at[piece]))
        copies[-1].start()
    for copy in copies:
        copy.wait()


def finish(name, own, near, far, start, rows, result=None):
    chained = result is not None
    pieces = 4
    return pl.pallas_call(
        functools.partial(finish_kernel, start, pieces, chained),
        out_shape=jax.ShapeDtypeStruct((rows, own.shape[1]), F32),
        in_specs=[VMEM] * 3 + [HBM] * chained,
        out_specs=HBM,
        scratch_shapes=[pltpu.VMEM(far.shape, F32), pltpu.SemaphoreType.DMA((pieces,))],
        input_output_aliases={3: 0} if chained else {},
        compiler_params=params(16),
        cost_estimate=CHEAP,
        name=name,
    )(own, near, far, *([result] if chained else []))


def slot_order(block_word, block_docs, live, position, own_blocks, devices):
    slot = jnp.arange(block_word.shape[0], dtype=jnp.int32)
    local = jnp.mod(block_word - (position - 1) * own_blocks, own_blocks * devices)
    side = local // own_blocks
    inner = local - side * own_blocks
    even = position % 2 == 0
    group = jnp.where(side == 1, 0, jnp.where((side == 0) == even, 2, 1))
    key = jnp.where(slot < live, group * own_blocks + inner, DEAD)
    rank_key = key * 64 + slot
    rank = jnp.sum((rank_key[None, :] < rank_key[:, None]).astype(jnp.int32), axis=1)
    code = slot + inner * 64 + block_docs * 1024
    order = jnp.sum(jnp.where(rank[:, None] == slot[None, :], code[:, None], 0), axis=0)
    marks = jnp.arange(3 * own_blocks + 1, dtype=jnp.int32)
    bounds = jnp.sum((key[None, :] < marks[:, None]).astype(jnp.int32), axis=1)
    return order, bounds


def on_device(block_count_values, word_factor, doc_factor, block_word, block_docs, block_count):
    devices = lax.axis_size("docs")
    position = lax.axis_index("docs")
    edge = block_count_values.shape[1]
    rows = word_factor.shape[0]
    own_blocks = rows // edge
    split = own_blocks // 2
    half = split * edge
    marks = (0, own_blocks, 2 * own_blocks, 2 * own_blocks + split, 3 * own_blocks)
    partner_route = [(i, i ^ 1) for i in range(devices)]
    cross_route = [(i, (i + 1) % devices if i % 2 else (i - 1) % devices) for i in range(devices)]

    def across(block):
        return lax.ppermute(block, "docs", cross_route)

    there = across(word_factor)
    partner = lax.ppermute(word_factor, "docs", partner_route)
    order, bounds = slot_order(
        block_word, block_docs, block_count[0], position, own_blocks, devices
    )
    counts = pltpu.with_memory_space_constraint(block_count_values, pltpu.HBM)
    run = functools.partial(word_terms, bounds=bounds, counts=counts, docs=doc_factor)
    own, kept = run("own", order=order, words=word_factor, marks=marks[0:2])
    near, kept = run("partner", order=order, words=partner, marks=marks[1:3], kept=kept)
    order, near = lax.optimization_barrier((order, near))
    near = lax.ppermute(near, "docs", partner_route)
    far_a, kept = run("cross_a", order=order, words=there, marks=marks[2:4], kept=kept, part=(0, split))
    order, far_a = lax.optimization_barrier((order, far_a.astype(F16)))
    far_a = across(far_a)
    far_b, kept = run(
        "cross_b", order=order, words=there, marks=marks[3:5], kept=kept, part=(split, own_blocks)
    )
    order, far_b, far_a = lax.optimization_barrier((order, far_b.astype(F16), far_a))
    far_b = across(far_b)
    document_gradient = doc_terms(
        order,
        bounds,
        kept,
        (word_factor, partner, there),
        (0, own_blocks, 2 * own_blocks, 3 * own_blocks),
        doc_factor.shape[1],
    )
    document_gradient, near = lax.optimization_barrier((document_gradient, near))
    result = finish("finish_a", own, near, far_a.astype(F32), 0, rows)
    result, far_b = lax.optimization_barrier((result, far_b))
    result = finish("finish_b", own, near, far_b.astype(F32), half, rows, result)
    return (result, document_gradient)


def solution(mesh):
    placed = (
        P("docs", None, None),
        P("docs", None),
        P(None, "docs"),
        P("docs"),
        P("docs"),
        P("docs"),
    )
    return jax.shard_map(
        on_device,
        mesh=mesh,
        in_specs=placed,
        out_specs=(P("docs", None), P(None, "docs")),
        check_vma=False,
    )
```

```python
import functools

import jax
import jax.numpy as jnp
from jax import lax
from jax.experimental import pallas as pl
from jax.experimental.pallas import tpu as pltpu
from jax.sharding import PartitionSpec as P

F32 = jnp.float32
BF16 = jnp.bfloat16
F16 = jnp.float16
VMEM = pl.BlockSpec(memory_space=pltpu.VMEM)
SMEM = pl.BlockSpec(memory_space=pltpu.SMEM)
HBM = pl.BlockSpec(memory_space=pltpu.HBM)
DEAD = 1 << 10
GROUP = 4
RING = 2 * GROUP
CHEAP = pl.CostEstimate(flops=1, bytes_accessed=1, transcendentals=0)


def params(megabytes):
    return pltpu.CompilerParams(vmem_limit_bytes=megabytes << 20)


def block_at(index, edge):
    return pl.ds(pl.multiple_of(index * edge, edge), edge)


def code_parts(code):
    return code & 63, (code >> 6) & 15, code >> 10


def word_kernel(spec, order, bounds, counts, words, docs, *refs):
    edge, first_mark, last_mark, base, chained = spec
    if chained:
        refs = refs[1:]
    grad, kept, held, staged, sems, out_sems = refs
    first, last = bounds[first_mark], bounds[last_mark]

    top = order.shape[0] - 1
    steps = (last - first + GROUP - 1) // GROUP

    def fetch(place):
        slot, _, _ = code_parts(order[jnp.minimum(place, top)])
        return pltpu.make_async_copy(counts.at[slot], held.at[place], sems.at[place])

    def keep(place, spot):
        return pltpu.make_async_copy(staged.at[spot], kept.at[place], out_sems.at[spot])

    @pl.loop(first, first + steps * GROUP)
    def _(place):
        fetch(place).start()

    grad[...] = jnp.zeros_like(grad)

    @pl.loop(0, steps)
    def _(step):
        start = first + GROUP * step
        half = (step & 1) * GROUP
        for g in range(GROUP):
            fetch(start + g).wait()

        @pl.when(step > 1)
        def _():
            for g in range(GROUP):
                keep(start + g - 2 * GROUP, half + g).wait()

        parts = [code_parts(order[jnp.minimum(start + g, last - 1)]) for g in range(GROUP)]
        rows = [block_at(word - base, edge) for _, word, _ in parts]
        cols = [block_at(doc, edge) for _, _, doc in parts]
        products = [
            jnp.dot(words[r, :], docs[:, c], preferred_element_type=F32) for r, c in zip(rows, cols)
        ]
        excess = []
        for g in range(GROUP):
            ratio = held[start + g].astype(F32) / products[g]
            one = (1.0 - ratio).astype(BF16)
            if g:
                one = jnp.where(start + g < last, one, jnp.zeros_like(one))
            excess.append(one)
            staged[half + g] = one
        terms = [
            lax.dot_general(e, docs[:, c], (((1,), (1,)), ((), ())), preferred_element_type=F32)
            for e, c in zip(excess, cols)
        ]
        for g in range(GROUP):
            grad[rows[g], :] += terms[g]
        for g in range(GROUP):
            keep(start + g, half + g).start()

    @pl.loop(GROUP * jnp.maximum(steps - 2, 0), GROUP * steps)
    def _(place):
        keep(first + place, place & (RING - 1)).wait()


def word_terms(name, order, bounds, counts, words, docs, marks, base=0, kept=None):
    slots, edge, _ = counts.shape
    chained = kept is not None
    spec = (edge, marks[0], marks[1], base, chained)
    return pl.pallas_call(
        functools.partial(word_kernel, spec),
        out_shape=[
            jax.ShapeDtypeStruct(words.shape, F32),
            pltpu.HBM((slots + GROUP, edge, edge), BF16),
        ],
        in_specs=[SMEM, SMEM, HBM, VMEM, VMEM] + [HBM] * chained,
        out_specs=[VMEM, HBM],
        scratch_shapes=[
            pltpu.VMEM((slots + GROUP, edge, edge), counts.dtype),
            pltpu.VMEM((RING, edge, edge), BF16),
            pltpu.SemaphoreType.DMA((slots + GROUP,)),
            pltpu.SemaphoreType.DMA((RING,)),
        ],
        input_output_aliases={5: 1} if chained else {},
        compiler_params=params(20),
        cost_estimate=CHEAP,
        name=name,
    )(order, bounds, counts, words, docs, *([kept] if chained else []))


def doc_kernel(spec, order, bounds, kept, *refs):
    edge, marks = spec
    sides, (grad, words, held, side_sems, sems) = refs[:-5], refs[-5:]
    starts = [sum(side.shape[0] for side in sides[:i]) for i in range(len(sides))]
    blocks = sides[0].shape[0] // edge
    total = bounds[marks[-1]]
    steps = (total + GROUP - 1) // GROUP
    empty = kept.shape[0]
    loads = [
        pltpu.make_async_copy(side, words.at[pl.ds(starts[i], side.shape[0])], side_sems.at[i])
        for i, side in enumerate(sides)
    ]
    for load in loads:
        load.start()

    def fetch(place):
        return pltpu.make_async_copy(kept.at[place], held.at[place], sems.at[place])

    @pl.loop(0, steps * GROUP)
    def _(place):
        fetch(place).start()

    held[empty] = jnp.zeros(held.shape[1:], held.dtype)
    grad[...] = jnp.zeros_like(grad)
    for load in loads:
        load.wait()

    def side_of(place):
        return sum((place >= bounds[mark]).astype(jnp.int32) for mark in marks[1:-1])

    @pl.loop(0, steps)
    def _(step):
        start = GROUP * step
        for g in range(GROUP):
            fetch(start + g).wait()
        cols, terms = [], []
        for g in range(GROUP):
            place = jnp.minimum(start + g, total - 1)
            _, word, doc = code_parts(order[place])
            one = held[jnp.where(start + g < total, place, empty)]
            cols.append(block_at(doc, edge))
            terms.append(
                lax.dot_general(
                    words[block_at(word + side_of(place) * blocks, edge), :],
                    one,
                    (((0,), (0,)), ((), ())),
                    preferred_element_type=F32,
                )
            )
        for c, term in zip(cols, terms):
            grad[:, c] += term


def doc_terms(order, bounds, kept, sides, marks, width):
    spots, edge, _ = kept.shape
    rank = sides[0].shape[1]
    return pl.pallas_call(
        functools.partial(doc_kernel, (edge, marks)),
        out_shape=jax.ShapeDtypeStruct((rank, width), F32),
        in_specs=[SMEM, SMEM, HBM] + [pl.BlockSpec(memory_space=pl.ANY)] * len(sides),
        out_specs=VMEM,
        scratch_shapes=[
            pltpu.VMEM((sum(side.shape[0] for side in sides), rank), BF16),
            pltpu.VMEM((spots + 1, edge, edge), BF16),
            pltpu.SemaphoreType.DMA((len(sides),)),
            pltpu.SemaphoreType.DMA((spots,)),
        ],
        compiler_params=params(20),
        cost_estimate=CHEAP,
        name="docs",
    )(order, bounds, pltpu.with_memory_space_constraint(kept, pltpu.HBM), *sides)


def finish_kernel(start, pieces, chained, *refs):
    own, near, far = refs[:3]
    out, sums, sems = refs[-3:]
    rows = far.shape[0] // pieces
    copies = []
    for piece in range(pieces):
        here = pl.ds(piece * rows, rows)
        there = pl.ds(start + piece * rows, rows)
        sums[here, :] = own[there, :] + near[there, :] + far[here, :]
        copies.append(pltpu.make_async_copy(sums.at[here], out.at[there], sems.at[piece]))
        copies[-1].start()
    for copy in copies:
        copy.wait()


def finish(name, own, near, far, start, rows, result=None):
    chained = result is not None
    pieces = 4
    return pl.pallas_call(
        functools.partial(finish_kernel, start, pieces, chained),
        out_shape=jax.ShapeDtypeStruct((rows, own.shape[1]), F32),
        in_specs=[VMEM] * 3 + [HBM] * chained,
        out_specs=HBM,
        scratch_shapes=[pltpu.VMEM(far.shape, F32), pltpu.SemaphoreType.DMA((pieces,))],
        input_output_aliases={3: 0} if chained else {},
        compiler_params=params(16),
        cost_estimate=CHEAP,
        name=name,
    )(own, near, far, *([result] if chained else []))


def slot_order(block_word, block_docs, live, position, own_blocks, devices):
    slot = jnp.arange(block_word.shape[0], dtype=jnp.int32)
    local = jnp.mod(block_word - (position - 1) * own_blocks, own_blocks * devices)
    side = local // own_blocks
    inner = local - side * own_blocks
    even = position % 2 == 0
    group = jnp.where(side == 1, 0, jnp.where((side == 0) == even, 2, 1))
    key = jnp.where(slot < live, group * own_blocks + inner, DEAD)
    rank_key = key * 64 + slot
    rank = jnp.sum((rank_key[None, :] < rank_key[:, None]).astype(jnp.int32), axis=1)
    code = slot + inner * 64 + block_docs * 1024
    order = jnp.sum(jnp.where(rank[:, None] == slot[None, :], code[:, None], 0), axis=0)
    marks = jnp.arange(3 * own_blocks + 1, dtype=jnp.int32)
    bounds = jnp.sum((key[None, :] < marks[:, None]).astype(jnp.int32), axis=1)
    return order, bounds


def on_device(block_count_values, word_factor, doc_factor, block_word, block_docs, block_count):
    devices = lax.axis_size("docs")
    position = lax.axis_index("docs")
    edge = block_count_values.shape[1]
    rows = word_factor.shape[0]
    own_blocks = rows // edge
    split = own_blocks // 2
    half = split * edge
    marks = (0, own_blocks, 2 * own_blocks, 2 * own_blocks + split, 3 * own_blocks)
    partner_route = [(i, i ^ 1) for i in range(devices)]
    cross_route = [(i, (i + 1) % devices if i % 2 else (i - 1) % devices) for i in range(devices)]

    def across(block):
        return lax.ppermute(block, "docs", cross_route)

    half_a, half_b, word_factor = lax.optimization_barrier(
        (word_factor[:half], word_factor[half:], word_factor)
    )
    there_a, there_b = across(half_a), across(half_b)
    partner = lax.ppermute(word_factor, "docs", partner_route)
    order, bounds = slot_order(
        block_word, block_docs, block_count[0], position, own_blocks, devices
    )
    counts = pltpu.with_memory_space_constraint(block_count_values, pltpu.HBM)
    run = functools.partial(word_terms, bounds=bounds, counts=counts, docs=doc_factor)
    own, kept = run("own", order=order, words=word_factor, marks=marks[0:2])
    near, kept = run("partner", order=order, words=partner, marks=marks[1:3], kept=kept)
    order, near = lax.optimization_barrier((order, near.astype(F16)))
    near = lax.ppermute(near, "docs", partner_route)
    far_a, kept = run("cross_a", order=order, words=there_a, marks=marks[2:4], kept=kept)
    order, far_a = lax.optimization_barrier((order, far_a.astype(F16)))
    far_a = across(far_a)
    far_b, kept = run(
        "cross_b", order=order, words=there_b, marks=marks[3:5], kept=kept, base=split
    )
    order, far_b = lax.optimization_barrier((order, far_b.astype(F16)))
    far_b = across(far_b)
    document_gradient = doc_terms(
        order,
        bounds,
        kept,
        (word_factor, partner, there_a, there_b),
        (0, own_blocks, 2 * own_blocks, 3 * own_blocks),
        doc_factor.shape[1],
    )
    document_gradient, near = lax.optimization_barrier((document_gradient, near))
    near = near.astype(F32)
    result = finish("finish_a", own, near, far_a.astype(F32), 0, rows)
    result, far_b = lax.optimization_barrier((result, far_b))
    result = finish("finish_b", own, near, far_b.astype(F32), half, rows, result)
    return (result, document_gradient)


def solution(mesh):
    placed = (
        P("docs", None, None),
        P("docs", None),
        P(None, "docs"),
        P("docs"),
        P("docs"),
        P("docs"),
    )
    return jax.shard_map(
        on_device,
        mesh=mesh,
        in_specs=placed,
        out_specs=(P("docs", None), P(None, "docs")),
        check_vma=False,
    )
```

```python
import functools

import jax
import jax.numpy as jnp
from jax import lax
from jax.experimental import pallas as pl
from jax.experimental.pallas import tpu as pltpu
from jax.sharding import PartitionSpec as P

F32 = jnp.float32
BF16 = jnp.bfloat16
F16 = jnp.float16
VMEM = pl.BlockSpec(memory_space=pltpu.VMEM)
SMEM = pl.BlockSpec(memory_space=pltpu.SMEM)
HBM = pl.BlockSpec(memory_space=pltpu.HBM)
DEAD = 1 << 10
GROUP = 4
RING = 2 * GROUP
CHEAP = pl.CostEstimate(flops=1, bytes_accessed=1, transcendentals=0)


def params(megabytes):
    return pltpu.CompilerParams(vmem_limit_bytes=megabytes << 20)


def block_at(index, edge):
    return pl.ds(pl.multiple_of(index * edge, edge), edge)


def code_parts(code):
    return code & 63, (code >> 6) & 15, code >> 10


def halves_kernel(split, pieces, source, low, high, staged, in_sems, out_sems):
    rows = source.shape[0] // pieces
    loads, stores = [], []
    for piece in range(pieces):
        here = pl.ds(piece * rows, rows)
        target = low if piece * rows < split else high
        there = pl.ds(piece * rows - (0 if piece * rows < split else split), rows)
        loads.append(pltpu.make_async_copy(source.at[here], staged.at[here], in_sems.at[piece]))
        stores.append(
            pltpu.make_async_copy(staged.at[here], target.at[there], out_sems.at[piece])
        )
        loads[-1].start()
    for load, store in zip(loads, stores):
        load.wait()
        store.start()
    for store in stores:
        store.wait()


def halves(block, split, pieces):
    rows, width = block.shape
    return pl.pallas_call(
        functools.partial(halves_kernel, split, pieces),
        out_shape=[
            pltpu.HBM((split, width), block.dtype),
            pltpu.HBM((rows - split, width), block.dtype),
        ],
        in_specs=[HBM],
        out_specs=[HBM, HBM],
        scratch_shapes=[
            pltpu.VMEM(block.shape, block.dtype),
            pltpu.SemaphoreType.DMA((pieces,)),
            pltpu.SemaphoreType.DMA((pieces,)),
        ],
        compiler_params=params(4),
        cost_estimate=CHEAP,
        name="halves",
    )(pltpu.with_memory_space_constraint(block, pltpu.HBM))


def word_kernel(spec, order, bounds, counts, words, docs, *refs):
    edge, first_mark, last_mark, base, chained = spec
    if chained:
        refs = refs[1:]
    grad, kept, held, staged, sems, out_sems = refs
    first, last = bounds[first_mark], bounds[last_mark]

    top = order.shape[0] - 1
    steps = (last - first + GROUP - 1) // GROUP

    def fetch(place):
        slot, _, _ = code_parts(order[jnp.minimum(place, top)])
        return pltpu.make_async_copy(counts.at[slot], held.at[place], sems.at[place])

    def keep(place, spot):
        return pltpu.make_async_copy(staged.at[spot], kept.at[place], out_sems.at[spot])

    @pl.loop(first, first + steps * GROUP)
    def _(place):
        fetch(place).start()

    grad[...] = jnp.zeros_like(grad)

    @pl.loop(0, steps)
    def _(step):
        start = first + GROUP * step
        half = (step & 1) * GROUP
        for g in range(GROUP):
            fetch(start + g).wait()

        @pl.when(step > 1)
        def _():
            for g in range(GROUP):
                keep(start + g - 2 * GROUP, half + g).wait()

        parts = [code_parts(order[jnp.minimum(start + g, last - 1)]) for g in range(GROUP)]
        rows = [block_at(word - base, edge) for _, word, _ in parts]
        cols = [block_at(doc, edge) for _, _, doc in parts]
        products = [
            jnp.dot(words[r, :], docs[:, c], preferred_element_type=F32) for r, c in zip(rows, cols)
        ]
        excess = []
        for g in range(GROUP):
            ratio = held[start + g].astype(F32) / products[g]
            one = (1.0 - ratio).astype(BF16)
            if g:
                one = jnp.where(start + g < last, one, jnp.zeros_like(one))
            excess.append(one)
            staged[half + g] = one
        terms = [
            lax.dot_general(e, docs[:, c], (((1,), (1,)), ((), ())), preferred_element_type=F32)
            for e, c in zip(excess, cols)
        ]
        for g in range(GROUP):
            grad[rows[g], :] += terms[g]
        for g in range(GROUP):
            keep(start + g, half + g).start()

    @pl.loop(GROUP * jnp.maximum(steps - 2, 0), GROUP * steps)
    def _(place):
        keep(first + place, place & (RING - 1)).wait()


def word_terms(name, order, bounds, counts, words, docs, marks, base=0, kept=None):
    slots, edge, _ = counts.shape
    chained = kept is not None
    spec = (edge, marks[0], marks[1], base, chained)
    return pl.pallas_call(
        functools.partial(word_kernel, spec),
        out_shape=[
            jax.ShapeDtypeStruct(words.shape, F32),
            pltpu.HBM((slots + GROUP, edge, edge), BF16),
        ],
        in_specs=[SMEM, SMEM, HBM, VMEM, VMEM] + [HBM] * chained,
        out_specs=[VMEM, HBM],
        scratch_shapes=[
            pltpu.VMEM((slots + GROUP, edge, edge), counts.dtype),
            pltpu.VMEM((RING, edge, edge), BF16),
            pltpu.SemaphoreType.DMA((slots + GROUP,)),
            pltpu.SemaphoreType.DMA((RING,)),
        ],
        input_output_aliases={5: 1} if chained else {},
        compiler_params=params(20),
        cost_estimate=CHEAP,
        name=name,
    )(order, bounds, counts, words, docs, *([kept] if chained else []))


def doc_kernel(spec, order, bounds, kept, *refs):
    edge, marks = spec
    sides, (grad, words, held, side_sems, sems) = refs[:-5], refs[-5:]
    starts = [sum(side.shape[0] for side in sides[:i]) for i in range(len(sides))]
    blocks = sides[0].shape[0] // edge
    total = bounds[marks[-1]]
    steps = (total + GROUP - 1) // GROUP
    empty = kept.shape[0]
    loads = [
        pltpu.make_async_copy(side, words.at[pl.ds(starts[i], side.shape[0])], side_sems.at[i])
        for i, side in enumerate(sides)
    ]
    for load in loads:
        load.start()

    def fetch(place):
        return pltpu.make_async_copy(kept.at[place], held.at[place], sems.at[place])

    @pl.loop(0, steps * GROUP)
    def _(place):
        fetch(place).start()

    held[empty] = jnp.zeros(held.shape[1:], held.dtype)
    grad[...] = jnp.zeros_like(grad)
    for load in loads:
        load.wait()

    def side_of(place):
        return sum((place >= bounds[mark]).astype(jnp.int32) for mark in marks[1:-1])

    @pl.loop(0, steps)
    def _(step):
        start = GROUP * step
        for g in range(GROUP):
            fetch(start + g).wait()
        cols, terms = [], []
        for g in range(GROUP):
            place = jnp.minimum(start + g, total - 1)
            _, word, doc = code_parts(order[place])
            one = held[jnp.where(start + g < total, place, empty)]
            cols.append(block_at(doc, edge))
            terms.append(
                lax.dot_general(
                    words[block_at(word + side_of(place) * blocks, edge), :],
                    one,
                    (((0,), (0,)), ((), ())),
                    preferred_element_type=F32,
                )
            )
        for c, term in zip(cols, terms):
            grad[:, c] += term


def doc_terms(order, bounds, kept, sides, marks, width):
    spots, edge, _ = kept.shape
    rank = sides[0].shape[1]
    return pl.pallas_call(
        functools.partial(doc_kernel, (edge, marks)),
        out_shape=jax.ShapeDtypeStruct((rank, width), F32),
        in_specs=[SMEM, SMEM, HBM] + [pl.BlockSpec(memory_space=pl.ANY)] * len(sides),
        out_specs=VMEM,
        scratch_shapes=[
            pltpu.VMEM((sum(side.shape[0] for side in sides), rank), BF16),
            pltpu.VMEM((spots + 1, edge, edge), BF16),
            pltpu.SemaphoreType.DMA((len(sides),)),
            pltpu.SemaphoreType.DMA((spots,)),
        ],
        compiler_params=params(20),
        cost_estimate=CHEAP,
        name="docs",
    )(order, bounds, pltpu.with_memory_space_constraint(kept, pltpu.HBM), *sides)


def finish_kernel(start, pieces, chained, *refs):
    own, near, far = refs[:3]
    out, sums, sems = refs[-3:]
    rows = far.shape[0] // pieces
    copies = []
    for piece in range(pieces):
        here = pl.ds(piece * rows, rows)
        there = pl.ds(start + piece * rows, rows)
        sums[here, :] = own[there, :] + near[there, :] + far[here, :]
        copies.append(pltpu.make_async_copy(sums.at[here], out.at[there], sems.at[piece]))
        copies[-1].start()
    for copy in copies:
        copy.wait()


def finish(name, own, near, far, start, rows, result=None):
    chained = result is not None
    pieces = max(far.shape[0] // 256, 1)
    return pl.pallas_call(
        functools.partial(finish_kernel, start, pieces, chained),
        out_shape=jax.ShapeDtypeStruct((rows, own.shape[1]), F32),
        in_specs=[VMEM] * 3 + [HBM] * chained,
        out_specs=HBM,
        scratch_shapes=[pltpu.VMEM(far.shape, F32), pltpu.SemaphoreType.DMA((pieces,))],
        input_output_aliases={3: 0} if chained else {},
        compiler_params=params(16),
        cost_estimate=CHEAP,
        name=name,
    )(own, near, far, *([result] if chained else []))


def slot_order(block_word, block_docs, live, position, own_blocks, devices):
    slot = jnp.arange(block_word.shape[0], dtype=jnp.int32)
    local = jnp.mod(block_word - (position - 1) * own_blocks, own_blocks * devices)
    side = local // own_blocks
    inner = local - side * own_blocks
    even = position % 2 == 0
    group = jnp.where(side == 1, 0, jnp.where((side == 0) == even, 2, 1))
    key = jnp.where(slot < live, group * own_blocks + inner, DEAD)
    rank_key = key * 64 + slot
    rank = jnp.sum((rank_key[None, :] < rank_key[:, None]).astype(jnp.int32), axis=1)
    code = slot + inner * 64 + block_docs * 1024
    order = jnp.sum(jnp.where(rank[:, None] == slot[None, :], code[:, None], 0), axis=0)
    marks = jnp.arange(3 * own_blocks + 1, dtype=jnp.int32)
    bounds = jnp.sum((key[None, :] < marks[:, None]).astype(jnp.int32), axis=1)
    return order, bounds


def on_device(block_count_values, word_factor, doc_factor, block_word, block_docs, block_count):
    devices = lax.axis_size("docs")
    position = lax.axis_index("docs")
    edge = block_count_values.shape[1]
    rows = word_factor.shape[0]
    own_blocks = rows // edge
    split = own_blocks // 2
    half = split * edge
    marks = (0, own_blocks, 2 * own_blocks, 2 * own_blocks + split, 3 * own_blocks)
    partner_route = [(i, i ^ 1) for i in range(devices)]
    cross_route = [(i, (i + 1) % devices if i % 2 else (i - 1) % devices) for i in range(devices)]

    def across(block):
        return lax.ppermute(block, "docs", cross_route)

    half_a, half_b = halves(word_factor, half, own_blocks)
    half_a, half_b, word_factor = lax.optimization_barrier((half_a, half_b, word_factor))
    there_a, there_b = across(half_a), across(half_b)
    partner = lax.ppermute(word_factor, "docs", partner_route)
    order, bounds = slot_order(
        block_word, block_docs, block_count[0], position, own_blocks, devices
    )
    counts = pltpu.with_memory_space_constraint(block_count_values, pltpu.HBM)
    run = functools.partial(word_terms, bounds=bounds, counts=counts, docs=doc_factor)
    own, kept = run("own", order=order, words=word_factor, marks=marks[0:2])
    near, kept = run("partner", order=order, words=partner, marks=marks[1:3], kept=kept)
    order, near = lax.optimization_barrier((order, near.astype(F16)))
    near = lax.ppermute(near, "docs", partner_route)
    far_a, kept = run("cross_a", order=order, words=there_a, marks=marks[2:4], kept=kept)
    order, far_a = lax.optimization_barrier((order, far_a.astype(F16)))
    far_a = across(far_a)
    far_b, kept = run(
        "cross_b", order=order, words=there_b, marks=marks[3:5], kept=kept, base=split
    )
    order, far_b = lax.optimization_barrier((order, far_b.astype(F16)))
    far_b = across(far_b)
    document_gradient = doc_terms(
        order,
        bounds,
        kept,
        (word_factor, partner, there_a, there_b),
        (0, own_blocks, 2 * own_blocks, 3 * own_blocks),
        doc_factor.shape[1],
    )
    document_gradient, near = lax.optimization_barrier((document_gradient, near))
    near = near.astype(F32)
    result = finish("finish_a", own, near, far_a.astype(F32), 0, rows)
    result, far_b = lax.optimization_barrier((result, far_b))
    result = finish("finish_b", own, near, far_b.astype(F32), half, rows, result)
    return (result, document_gradient)


def solution(mesh):
    placed = (
        P("docs", None, None),
        P("docs", None),
        P(None, "docs"),
        P("docs"),
        P("docs"),
        P("docs"),
    )
    return jax.shard_map(
        on_device,
        mesh=mesh,
        in_specs=placed,
        out_specs=(P("docs", None), P(None, "docs")),
        check_vma=False,
    )
```

```python
import functools

import jax
import jax.numpy as jnp
from jax import lax
from jax.experimental import pallas as pl
from jax.experimental.pallas import tpu as pltpu
from jax.sharding import PartitionSpec as P

F32 = jnp.float32
BF16 = jnp.bfloat16
F16 = jnp.float16
VMEM = pl.BlockSpec(memory_space=pltpu.VMEM)
SMEM = pl.BlockSpec(memory_space=pltpu.SMEM)
HBM = pl.BlockSpec(memory_space=pltpu.HBM)
DEAD = 1 << 10
GROUP = 4
RING = 2 * GROUP
CHEAP = pl.CostEstimate(flops=1, bytes_accessed=1, transcendentals=0)


def params(megabytes):
    return pltpu.CompilerParams(vmem_limit_bytes=megabytes << 20)


def block_at(index, edge):
    return pl.ds(pl.multiple_of(index * edge, edge), edge)


def code_parts(code):
    return code & 63, (code >> 6) & 15, code >> 10


def halves_kernel(split, source, low, high, sems):
    copies = [
        pltpu.make_async_copy(source.at[pl.ds(0, split)], low, sems.at[0]),
        pltpu.make_async_copy(
            source.at[pl.ds(split, source.shape[0] - split)], high, sems.at[1]
        ),
    ]
    for copy in copies:
        copy.start()
    for copy in copies:
        copy.wait()


def halves(block, split):
    rows, width = block.shape
    return pl.pallas_call(
        functools.partial(halves_kernel, split),
        out_shape=[
            pltpu.VMEM((split, width), block.dtype),
            pltpu.VMEM((rows - split, width), block.dtype),
        ],
        in_specs=[HBM],
        out_specs=[VMEM, VMEM],
        scratch_shapes=[pltpu.SemaphoreType.DMA((2,))],
        compiler_params=params(4),
        cost_estimate=CHEAP,
        name="halves",
    )(pltpu.with_memory_space_constraint(block, pltpu.HBM))


def word_kernel(spec, order, bounds, counts, words, docs, *refs):
    edge, first_mark, last_mark, base, chained, loading = spec
    if chained:
        refs = refs[1:]
    grad, kept, held, staged, sems, out_sems = refs[:6]
    loads = []
    if loading:
        words_here, docs_here, load_sems = refs[6:]
        loads = [
            pltpu.make_async_copy(words, words_here, load_sems.at[0]),
            pltpu.make_async_copy(docs, docs_here, load_sems.at[1]),
        ]
        words, docs = words_here, docs_here
    for load in loads:
        load.start()
    first, last = bounds[first_mark], bounds[last_mark]

    top = order.shape[0] - 1
    steps = (last - first + GROUP - 1) // GROUP

    def fetch(place):
        slot, _, _ = code_parts(order[jnp.minimum(place, top)])
        return pltpu.make_async_copy(counts.at[slot], held.at[place], sems.at[place])

    def keep(place, spot):
        return pltpu.make_async_copy(staged.at[spot], kept.at[place], out_sems.at[spot])

    @pl.loop(first, first + steps * GROUP)
    def _(place):
        fetch(place).start()

    grad[...] = jnp.zeros_like(grad)
    for load in loads:
        load.wait()

    @pl.loop(0, steps)
    def _(step):
        start = first + GROUP * step
        half = (step & 1) * GROUP
        for g in range(GROUP):
            fetch(start + g).wait()

        @pl.when(step > 1)
        def _():
            for g in range(GROUP):
                keep(start + g - 2 * GROUP, half + g).wait()

        parts = [code_parts(order[jnp.minimum(start + g, last - 1)]) for g in range(GROUP)]
        rows = [block_at(word - base, edge) for _, word, _ in parts]
        cols = [block_at(doc, edge) for _, _, doc in parts]
        products = [
            jnp.dot(words[r, :], docs[:, c], preferred_element_type=F32) for r, c in zip(rows, cols)
        ]
        excess = []
        for g in range(GROUP):
            ratio = held[start + g].astype(F32) / products[g]
            one = (1.0 - ratio).astype(BF16)
            if g:
                one = jnp.where(start + g < last, one, jnp.zeros_like(one))
            excess.append(one)
            staged[half + g] = one
        terms = [
            lax.dot_general(e, docs[:, c], (((1,), (1,)), ((), ())), preferred_element_type=F32)
            for e, c in zip(excess, cols)
        ]
        for g in range(GROUP):
            grad[rows[g], :] += terms[g]
        for g in range(GROUP):
            keep(start + g, half + g).start()

    @pl.loop(GROUP * jnp.maximum(steps - 2, 0), GROUP * steps)
    def _(place):
        keep(first + place, place & (RING - 1)).wait()


def word_terms(name, order, bounds, counts, words, docs, marks, base=0, kept=None):
    slots, edge, _ = counts.shape
    chained = kept is not None
    loading = not chained
    spec = (edge, marks[0], marks[1], base, chained, loading)
    if loading:
        words, docs = (pltpu.with_memory_space_constraint(x, pltpu.HBM) for x in (words, docs))
    return pl.pallas_call(
        functools.partial(word_kernel, spec),
        out_shape=[
            jax.ShapeDtypeStruct(words.shape, F32),
            pltpu.HBM((slots + GROUP, edge, edge), BF16),
        ],
        in_specs=[SMEM, SMEM, HBM] + [HBM if loading else VMEM] * 2 + [HBM] * chained,
        out_specs=[VMEM, HBM],
        scratch_shapes=[
            pltpu.VMEM((slots + GROUP, edge, edge), counts.dtype),
            pltpu.VMEM((RING, edge, edge), BF16),
            pltpu.SemaphoreType.DMA((slots + GROUP,)),
            pltpu.SemaphoreType.DMA((RING,)),
        ]
        + loading
        * [
            pltpu.VMEM(words.shape, words.dtype),
            pltpu.VMEM(docs.shape, docs.dtype),
            pltpu.SemaphoreType.DMA((2,)),
        ],
        input_output_aliases={5: 1} if chained else {},
        compiler_params=params(24 if loading else 20),
        cost_estimate=CHEAP,
        name=name,
    )(order, bounds, counts, words, docs, *([kept] if chained else []))


def doc_kernel(spec, order, bounds, kept, *refs):
    edge, marks = spec
    sides, (grad, words, held, side_sems, sems) = refs[:-5], refs[-5:]
    starts = [sum(side.shape[0] for side in sides[:i]) for i in range(len(sides))]
    blocks = sides[0].shape[0] // edge
    total = bounds[marks[-1]]
    steps = (total + GROUP - 1) // GROUP
    empty = kept.shape[0]
    loads = [
        pltpu.make_async_copy(side, words.at[pl.ds(starts[i], side.shape[0])], side_sems.at[i])
        for i, side in enumerate(sides)
    ]
    for load in loads:
        load.start()

    def fetch(place):
        return pltpu.make_async_copy(kept.at[place], held.at[place], sems.at[place])

    @pl.loop(0, steps * GROUP)
    def _(place):
        fetch(place).start()

    held[empty] = jnp.zeros(held.shape[1:], held.dtype)
    grad[...] = jnp.zeros_like(grad)
    for load in loads:
        load.wait()

    def side_of(place):
        return sum((place >= bounds[mark]).astype(jnp.int32) for mark in marks[1:-1])

    @pl.loop(0, steps)
    def _(step):
        start = GROUP * step
        for g in range(GROUP):
            fetch(start + g).wait()
        cols, terms = [], []
        for g in range(GROUP):
            place = jnp.minimum(start + g, total - 1)
            _, word, doc = code_parts(order[place])
            one = held[jnp.where(start + g < total, place, empty)]
            cols.append(block_at(doc, edge))
            terms.append(
                lax.dot_general(
                    words[block_at(word + side_of(place) * blocks, edge), :],
                    one,
                    (((0,), (0,)), ((), ())),
                    preferred_element_type=F32,
                )
            )
        for c, term in zip(cols, terms):
            grad[:, c] += term


def doc_terms(order, bounds, kept, sides, marks, width):
    spots, edge, _ = kept.shape
    rank = sides[0].shape[1]
    return pl.pallas_call(
        functools.partial(doc_kernel, (edge, marks)),
        out_shape=jax.ShapeDtypeStruct((rank, width), F32),
        in_specs=[SMEM, SMEM, HBM] + [pl.BlockSpec(memory_space=pl.ANY)] * len(sides),
        out_specs=VMEM,
        scratch_shapes=[
            pltpu.VMEM((sum(side.shape[0] for side in sides), rank), BF16),
            pltpu.VMEM((spots + 1, edge, edge), BF16),
            pltpu.SemaphoreType.DMA((len(sides),)),
            pltpu.SemaphoreType.DMA((spots,)),
        ],
        compiler_params=params(20),
        cost_estimate=CHEAP,
        name="docs",
    )(order, bounds, pltpu.with_memory_space_constraint(kept, pltpu.HBM), *sides)


def finish_kernel(start, pieces, chained, *refs):
    own, near, far = refs[:3]
    out, sums, sems = refs[-3:]
    rows = far.shape[0] // pieces
    copies = []
    for piece in range(pieces):
        here = pl.ds(piece * rows, rows)
        there = pl.ds(start + piece * rows, rows)
        sums[here, :] = own[there, :] + near[there, :] + far[here, :]
        copies.append(pltpu.make_async_copy(sums.at[here], out.at[there], sems.at[piece]))
        copies[-1].start()
    for copy in copies:
        copy.wait()


def finish(name, own, near, far, start, rows, result=None):
    chained = result is not None
    pieces = max(far.shape[0] // 256, 1)
    return pl.pallas_call(
        functools.partial(finish_kernel, start, pieces, chained),
        out_shape=jax.ShapeDtypeStruct((rows, own.shape[1]), F32),
        in_specs=[VMEM] * 3 + [HBM] * chained,
        out_specs=HBM,
        scratch_shapes=[pltpu.VMEM(far.shape, F32), pltpu.SemaphoreType.DMA((pieces,))],
        input_output_aliases={3: 0} if chained else {},
        compiler_params=params(16),
        cost_estimate=CHEAP,
        name=name,
    )(own, near, far, *([result] if chained else []))


def slot_order(block_word, block_docs, live, position, own_blocks, devices):
    slot = jnp.arange(block_word.shape[0], dtype=jnp.int32)
    local = jnp.mod(block_word - (position - 1) * own_blocks, own_blocks * devices)
    side = local // own_blocks
    inner = local - side * own_blocks
    even = position % 2 == 0
    group = jnp.where(side == 1, 0, jnp.where((side == 0) == even, 2, 1))
    key = jnp.where(slot < live, group * own_blocks + inner, DEAD)
    rank_key = key * 64 + slot
    rank = jnp.sum((rank_key[None, :] < rank_key[:, None]).astype(jnp.int32), axis=1)
    code = slot + inner * 64 + block_docs * 1024
    order = jnp.sum(jnp.where(rank[:, None] == slot[None, :], code[:, None], 0), axis=0)
    marks = jnp.arange(3 * own_blocks + 1, dtype=jnp.int32)
    bounds = jnp.sum((key[None, :] < marks[:, None]).astype(jnp.int32), axis=1)
    return order, bounds


def on_device(block_count_values, word_factor, doc_factor, block_word, block_docs, block_count):
    devices = lax.axis_size("docs")
    position = lax.axis_index("docs")
    edge = block_count_values.shape[1]
    rows = word_factor.shape[0]
    own_blocks = rows // edge
    split = own_blocks // 2
    half = split * edge
    marks = (0, own_blocks, 2 * own_blocks, 2 * own_blocks + split, 3 * own_blocks)
    partner_route = [(i, i ^ 1) for i in range(devices)]
    cross_route = [(i, (i + 1) % devices if i % 2 else (i - 1) % devices) for i in range(devices)]

    def across(block):
        return lax.ppermute(block, "docs", cross_route)

    half_a, half_b = halves(word_factor, half)
    half_a, half_b, word_factor = lax.optimization_barrier((half_a, half_b, word_factor))
    there_a, there_b = across(half_a), across(half_b)
    partner = lax.ppermute(word_factor, "docs", partner_route)
    order, bounds = slot_order(
        block_word, block_docs, block_count[0], position, own_blocks, devices
    )
    counts = pltpu.with_memory_space_constraint(block_count_values, pltpu.HBM)
    run = functools.partial(word_terms, bounds=bounds, counts=counts, docs=doc_factor)
    own, kept = run("own", order=order, words=word_factor, marks=marks[0:2])
    near, kept = run("partner", order=order, words=partner, marks=marks[1:3], kept=kept)
    order, near = lax.optimization_barrier((order, near.astype(F16)))
    near = lax.ppermute(near, "docs", partner_route)
    far_a, kept = run("cross_a", order=order, words=there_a, marks=marks[2:4], kept=kept)
    order, far_a = lax.optimization_barrier((order, far_a.astype(F16)))
    far_a = across(far_a)
    far_b, kept = run(
        "cross_b", order=order, words=there_b, marks=marks[3:5], kept=kept, base=split
    )
    order, far_b = lax.optimization_barrier((order, far_b.astype(F16)))
    far_b = across(far_b)
    document_gradient = doc_terms(
        order,
        bounds,
        kept,
        (word_factor, partner, there_a, there_b),
        (0, own_blocks, 2 * own_blocks, 3 * own_blocks),
        doc_factor.shape[1],
    )
    document_gradient, near = lax.optimization_barrier((document_gradient, near))
    near = near.astype(F32)
    result = finish("finish_a", own, near, far_a.astype(F32), 0, rows)
    result, far_b = lax.optimization_barrier((result, far_b))
    result = finish("finish_b", own, near, far_b.astype(F32), half, rows, result)
    return (result, document_gradient)


def solution(mesh):
    placed = (
        P("docs", None, None),
        P("docs", None),
        P(None, "docs"),
        P("docs"),
        P("docs"),
        P("docs"),
    )
    return jax.shard_map(
        on_device,
        mesh=mesh,
        in_specs=placed,
        out_specs=(P("docs", None), P(None, "docs")),
        check_vma=False,
    )
```

```python
import functools

import jax
import jax.numpy as jnp
from jax import lax
from jax.experimental import pallas as pl
from jax.experimental.pallas import tpu as pltpu
from jax.sharding import PartitionSpec as P

F32 = jnp.float32
BF16 = jnp.bfloat16
F16 = jnp.float16
VMEM = pl.BlockSpec(memory_space=pltpu.VMEM)
SMEM = pl.BlockSpec(memory_space=pltpu.SMEM)
HBM = pl.BlockSpec(memory_space=pltpu.HBM)
DEAD = 1 << 10
GROUP = 4
RING = 2 * GROUP
CHEAP = pl.CostEstimate(flops=1, bytes_accessed=1, transcendentals=0)


def params(megabytes):
    return pltpu.CompilerParams(vmem_limit_bytes=megabytes << 20)


def block_at(index, edge):
    return pl.ds(pl.multiple_of(index * edge, edge), edge)


def code_parts(code):
    return code & 63, (code >> 6) & 15, code >> 10


def cut_kernel(start, pieces, source, target, staged, in_sems, out_sems):
    rows = target.shape[0] // pieces
    loads, stores = [], []
    for piece in range(pieces):
        here = pl.ds(piece * rows, rows)
        there = pl.ds(start + piece * rows, rows)
        loads.append(pltpu.make_async_copy(source.at[there], staged.at[here], in_sems.at[piece]))
        stores.append(
            pltpu.make_async_copy(staged.at[here], target.at[here], out_sems.at[piece])
        )
        loads[-1].start()
    for load, store in zip(loads, stores):
        load.wait()
        store.start()
    for store in stores:
        store.wait()


def cut(name, block, start, rows, pieces):
    shape = (rows, block.shape[1])
    return pl.pallas_call(
        functools.partial(cut_kernel, start, pieces),
        out_shape=pltpu.HBM(shape, block.dtype),
        in_specs=[HBM],
        out_specs=HBM,
        scratch_shapes=[
            pltpu.VMEM(shape, block.dtype),
            pltpu.SemaphoreType.DMA((pieces,)),
            pltpu.SemaphoreType.DMA((pieces,)),
        ],
        compiler_params=params(4),
        cost_estimate=CHEAP,
        name=name,
    )(pltpu.with_memory_space_constraint(block, pltpu.HBM))


def word_kernel(spec, order, bounds, counts, words, docs, *refs):
    edge, first_mark, last_mark, base, chained, loading = spec
    if chained:
        refs = refs[1:]
    grad, kept, held, staged, sems, out_sems = refs[:6]
    loads = []
    if loading:
        words_here, docs_here, load_sems = refs[6:]
        loads = [
            pltpu.make_async_copy(words, words_here, load_sems.at[0]),
            pltpu.make_async_copy(docs, docs_here, load_sems.at[1]),
        ]
        words, docs = words_here, docs_here
    for load in loads:
        load.start()
    first, last = bounds[first_mark], bounds[last_mark]

    top = order.shape[0] - 1
    steps = (last - first + GROUP - 1) // GROUP

    def fetch(place):
        slot, _, _ = code_parts(order[jnp.minimum(place, top)])
        return pltpu.make_async_copy(counts.at[slot], held.at[place], sems.at[place])

    def keep(place, spot):
        return pltpu.make_async_copy(staged.at[spot], kept.at[place], out_sems.at[spot])

    @pl.loop(first, first + steps * GROUP)
    def _(place):
        fetch(place).start()

    grad[...] = jnp.zeros_like(grad)
    for load in loads:
        load.wait()

    @pl.loop(0, steps)
    def _(step):
        start = first + GROUP * step
        half = (step & 1) * GROUP
        for g in range(GROUP):
            fetch(start + g).wait()

        @pl.when(step > 1)
        def _():
            for g in range(GROUP):
                keep(start + g - 2 * GROUP, half + g).wait()

        parts = [code_parts(order[jnp.minimum(start + g, last - 1)]) for g in range(GROUP)]
        rows = [block_at(word - base, edge) for _, word, _ in parts]
        cols = [block_at(doc, edge) for _, _, doc in parts]
        products = [
            jnp.dot(words[r, :], docs[:, c], preferred_element_type=F32) for r, c in zip(rows, cols)
        ]
        excess = []
        for g in range(GROUP):
            ratio = held[start + g].astype(F32) / products[g]
            one = (1.0 - ratio).astype(BF16)
            if g:
                one = jnp.where(start + g < last, one, jnp.zeros_like(one))
            excess.append(one)
            staged[half + g] = one
        terms = [
            lax.dot_general(e, docs[:, c], (((1,), (1,)), ((), ())), preferred_element_type=F32)
            for e, c in zip(excess, cols)
        ]
        for g in range(GROUP):
            grad[rows[g], :] += terms[g]
        for g in range(GROUP):
            keep(start + g, half + g).start()

    @pl.loop(GROUP * jnp.maximum(steps - 2, 0), GROUP * steps)
    def _(place):
        keep(first + place, place & (RING - 1)).wait()


def word_terms(name, order, bounds, counts, words, docs, marks, base=0, kept=None):
    slots, edge, _ = counts.shape
    chained = kept is not None
    loading = not chained
    spec = (edge, marks[0], marks[1], base, chained, loading)
    if loading:
        words, docs = (pltpu.with_memory_space_constraint(x, pltpu.HBM) for x in (words, docs))
    return pl.pallas_call(
        functools.partial(word_kernel, spec),
        out_shape=[
            jax.ShapeDtypeStruct(words.shape, F32),
            pltpu.HBM((slots + GROUP, edge, edge), BF16),
        ],
        in_specs=[SMEM, SMEM, HBM] + [HBM if loading else VMEM] * 2 + [HBM] * chained,
        out_specs=[VMEM, HBM],
        scratch_shapes=[
            pltpu.VMEM((slots + GROUP, edge, edge), counts.dtype),
            pltpu.VMEM((RING, edge, edge), BF16),
            pltpu.SemaphoreType.DMA((slots + GROUP,)),
            pltpu.SemaphoreType.DMA((RING,)),
        ]
        + loading
        * [
            pltpu.VMEM(words.shape, words.dtype),
            pltpu.VMEM(docs.shape, docs.dtype),
            pltpu.SemaphoreType.DMA((2,)),
        ],
        input_output_aliases={5: 1} if chained else {},
        compiler_params=params(24 if loading else 20),
        cost_estimate=CHEAP,
        name=name,
    )(order, bounds, counts, words, docs, *([kept] if chained else []))


def doc_kernel(spec, order, bounds, kept, *refs):
    edge, marks = spec
    sides, (grad, words, held, side_sems, sems) = refs[:-5], refs[-5:]
    starts = [sum(side.shape[0] for side in sides[:i]) for i in range(len(sides))]
    blocks = sides[0].shape[0] // edge
    total = bounds[marks[-1]]
    steps = (total + GROUP - 1) // GROUP
    empty = kept.shape[0]
    loads = [
        pltpu.make_async_copy(side, words.at[pl.ds(starts[i], side.shape[0])], side_sems.at[i])
        for i, side in enumerate(sides)
    ]
    for load in loads:
        load.start()

    def fetch(place):
        return pltpu.make_async_copy(kept.at[place], held.at[place], sems.at[place])

    @pl.loop(0, steps * GROUP)
    def _(place):
        fetch(place).start()

    held[empty] = jnp.zeros(held.shape[1:], held.dtype)
    grad[...] = jnp.zeros_like(grad)
    for load in loads:
        load.wait()

    def side_of(place):
        return sum((place >= bounds[mark]).astype(jnp.int32) for mark in marks[1:-1])

    @pl.loop(0, steps)
    def _(step):
        start = GROUP * step
        for g in range(GROUP):
            fetch(start + g).wait()
        cols, terms = [], []
        for g in range(GROUP):
            place = jnp.minimum(start + g, total - 1)
            _, word, doc = code_parts(order[place])
            one = held[jnp.where(start + g < total, place, empty)]
            cols.append(block_at(doc, edge))
            terms.append(
                lax.dot_general(
                    words[block_at(word + side_of(place) * blocks, edge), :],
                    one,
                    (((0,), (0,)), ((), ())),
                    preferred_element_type=F32,
                )
            )
        for c, term in zip(cols, terms):
            grad[:, c] += term


def doc_terms(order, bounds, kept, sides, marks, width):
    spots, edge, _ = kept.shape
    rank = sides[0].shape[1]
    return pl.pallas_call(
        functools.partial(doc_kernel, (edge, marks)),
        out_shape=jax.ShapeDtypeStruct((rank, width), F32),
        in_specs=[SMEM, SMEM, HBM] + [pl.BlockSpec(memory_space=pl.ANY)] * len(sides),
        out_specs=VMEM,
        scratch_shapes=[
            pltpu.VMEM((sum(side.shape[0] for side in sides), rank), BF16),
            pltpu.VMEM((spots + 1, edge, edge), BF16),
            pltpu.SemaphoreType.DMA((len(sides),)),
            pltpu.SemaphoreType.DMA((spots,)),
        ],
        compiler_params=params(20),
        cost_estimate=CHEAP,
        name="docs",
    )(order, bounds, pltpu.with_memory_space_constraint(kept, pltpu.HBM), *sides)


def finish_kernel(start, pieces, chained, *refs):
    own, near, far = refs[:3]
    out, sums, sems = refs[-3:]
    rows = far.shape[0] // pieces
    copies = []
    for piece in range(pieces):
        here = pl.ds(piece * rows, rows)
        there = pl.ds(start + piece * rows, rows)
        sums[here, :] = own[there, :] + near[there, :] + far[here, :]
        copies.append(pltpu.make_async_copy(sums.at[here], out.at[there], sems.at[piece]))
        copies[-1].start()
    for copy in copies:
        copy.wait()


def finish(name, own, near, far, start, rows, result=None):
    chained = result is not None
    pieces = max(far.shape[0] // 256, 1)
    return pl.pallas_call(
        functools.partial(finish_kernel, start, pieces, chained),
        out_shape=jax.ShapeDtypeStruct((rows, own.shape[1]), F32),
        in_specs=[VMEM] * 3 + [HBM] * chained,
        out_specs=HBM,
        scratch_shapes=[pltpu.VMEM(far.shape, F32), pltpu.SemaphoreType.DMA((pieces,))],
        input_output_aliases={3: 0} if chained else {},
        compiler_params=params(16),
        cost_estimate=CHEAP,
        name=name,
    )(own, near, far, *([result] if chained else []))


def slot_order(block_word, block_docs, live, position, own_blocks, devices):
    slot = jnp.arange(block_word.shape[0], dtype=jnp.int32)
    local = jnp.mod(block_word - (position - 1) * own_blocks, own_blocks * devices)
    side = local // own_blocks
    inner = local - side * own_blocks
    even = position % 2 == 0
    group = jnp.where(side == 1, 0, jnp.where((side == 0) == even, 2, 1))
    key = jnp.where(slot < live, group * own_blocks + inner, DEAD)
    rank_key = key * 64 + slot
    rank = jnp.sum((rank_key[None, :] < rank_key[:, None]).astype(jnp.int32), axis=1)
    code = slot + inner * 64 + block_docs * 1024
    order = jnp.sum(jnp.where(rank[:, None] == slot[None, :], code[:, None], 0), axis=0)
    marks = jnp.arange(3 * own_blocks + 1, dtype=jnp.int32)
    bounds = jnp.sum((key[None, :] < marks[:, None]).astype(jnp.int32), axis=1)
    return order, bounds


def on_device(block_count_values, word_factor, doc_factor, block_word, block_docs, block_count):
    devices = lax.axis_size("docs")
    position = lax.axis_index("docs")
    edge = block_count_values.shape[1]
    rows = word_factor.shape[0]
    own_blocks = rows // edge
    split = own_blocks // 2
    half = split * edge
    marks = (0, own_blocks, 2 * own_blocks, 2 * own_blocks + split, 3 * own_blocks)
    partner_route = [(i, i ^ 1) for i in range(devices)]
    cross_route = [(i, (i + 1) % devices if i % 2 else (i - 1) % devices) for i in range(devices)]

    def across(block):
        return lax.ppermute(block, "docs", cross_route)

    partner = lax.ppermute(word_factor, "docs", partner_route)
    half_a = cut("cut_a", word_factor, 0, half, split)
    half_a, word_factor = lax.optimization_barrier((half_a, word_factor))
    there_a = across(half_a)
    half_b = cut("cut_b", word_factor, half, rows - half, own_blocks - split)
    half_b, word_factor = lax.optimization_barrier((half_b, word_factor))
    there_b = across(half_b)
    order, bounds = slot_order(
        block_word, block_docs, block_count[0], position, own_blocks, devices
    )
    counts = pltpu.with_memory_space_constraint(block_count_values, pltpu.HBM)
    run = functools.partial(word_terms, bounds=bounds, counts=counts, docs=doc_factor)
    own, kept = run("own", order=order, words=word_factor, marks=marks[0:2])
    near, kept = run("partner", order=order, words=partner, marks=marks[1:3], kept=kept)
    order, near = lax.optimization_barrier((order, near.astype(F16)))
    near = lax.ppermute(near, "docs", partner_route)
    far_a, kept = run("cross_a", order=order, words=there_a, marks=marks[2:4], kept=kept)
    order, far_a = lax.optimization_barrier((order, far_a.astype(F16)))
    far_a = across(far_a)
    far_b, kept = run(
        "cross_b", order=order, words=there_b, marks=marks[3:5], kept=kept, base=split
    )
    order, far_b = lax.optimization_barrier((order, far_b.astype(F16)))
    far_b = across(far_b)
    document_gradient = doc_terms(
        order,
        bounds,
        kept,
        (word_factor, partner, there_a, there_b),
        (0, own_blocks, 2 * own_blocks, 3 * own_blocks),
        doc_factor.shape[1],
    )
    document_gradient, near = lax.optimization_barrier((document_gradient, near))
    near = near.astype(F32)
    result = finish("finish_a", own, near, far_a.astype(F32), 0, rows)
    result, far_b = lax.optimization_barrier((result, far_b))
    result = finish("finish_b", own, near, far_b.astype(F32), half, rows, result)
    return (result, document_gradient)


def solution(mesh):
    placed = (
        P("docs", None, None),
        P("docs", None),
        P(None, "docs"),
        P("docs"),
        P("docs"),
        P("docs"),
    )
    return jax.shard_map(
        on_device,
        mesh=mesh,
        in_specs=placed,
        out_specs=(P("docs", None), P(None, "docs")),
        check_vma=False,
    )
```
